32 devices in a mesh: shard: 4 (over y, core), rep: 8 (over z, x).
Axes of the slice: x: 2, y: 2, z: 4, core: 2. Of those that a mesh axis runs over, the one named last changes fastest.
Arguments:
- inputs: bfloat16 [8, 1024, 512], P('rep', 'shard'), may hold values from -6 to 6
- w_in: bfloat16 [512, 2048], replicated, may hold values from -0.25 to 0.25
- grad_out: bfloat16 [8, 1024, 512], P('rep', 'shard'), may hold values from -6 to 6
- w_out: bfloat16 [512, 512], replicated, may hold values from -0.25 to 0.25
- dest: int32 [8, 1024], P('rep', 'shard'), may hold values from 0 to 3, as said below
- slot: int32 [8, 1024], P('rep', 'shard'), may hold values from 0 to 127, as said below
- slot_user: int32 [8, 2048], P('rep', 'shard'), may hold values from -1 to 3, as said below
- slot_time: int32 [8, 2048], P('rep', 'shard'), may hold values from 0 to 511, as said below
Outputs:
- grad_proj: bfloat16 [8, 1024, 2048], P('rep', 'shard')
- grad_w_out: float32 [512, 512], replicated
The draws below stay inside these ranges and needn't reach their ends.
Inputs may be any that keep to these rules, and one draw needn't show every extreme that they name: Events of one log shard with the same dest have distinct slots; at most 128 events of one log shard go to one owner, and in every group some owner receives exactly 128 from every log shard. `slot`: see dest. `slot_user`: owner o's slot s * 128 + t is -1 exactly when log shard s of the group sends no event with dest o and slot t. `slot_time`: distinct within one owner.
All inputs are finite; a program needn't handle non-finite values.
Results may differ from the reference program's by a relative error of at most 0.0076.
Values may be sent and summed in bfloat16 or wider, within the bound.
No kernel may reach another device: no remote copies, remote signals or barrier semaphores. Data moves between devices by JAX's collectives and lax.ppermute only.
A program may use at most 64 MiB of HBM per device.

```python
import math
import jax
import jax.numpy as jnp
from jax import lax

D = 512
HEADS = 4
E_DEV = 256
USERS = 4
SLOT = 128
CAP = 512
GROUP_EVENTS = 1024
N_SHARD = 4
N_REP = 8


def route_plan(key):
    base_key = jax.random.fold_in(key, 7)
    key_full, key_perm, key_order, key_user, key_time = jax.random.split(base_key, 5)
    share = E_DEV // N_SHARD
    pattern = jnp.tile(jnp.array([2, 1, 1, 0], jnp.int32), N_SHARD // 4) * share
    remainder = pattern[1:]
    full_owner = jax.random.randint(key_full, (N_REP,), 0, N_SHARD).astype(jnp.int32)
    perm_keys = jax.random.split(key_perm, N_REP * N_SHARD)
    perms = jax.vmap(lambda one: jax.random.permutation(one, N_SHARD - 1))(perm_keys).reshape(N_REP, N_SHARD, N_SHARD - 1)
    values = remainder[perms]
    others = (full_owner[:, None] + 1 + jnp.arange(N_SHARD - 1, dtype=jnp.int32)[None, :]) % N_SHARD
    owner_ids = jnp.arange(N_SHARD, dtype=jnp.int32)
    hits = (others[:, None, :, None] == owner_ids[None, None, None, :]).astype(jnp.int32)
    counts = jnp.sum(values[:, :, :, None] * hits, axis=2)
    counts = counts + (owner_ids[None, None, :] == full_owner[:, None, None]).astype(jnp.int32) * (2 * share)
    ends = jnp.cumsum(counts, axis=2)
    starts = ends - counts
    events = jnp.arange(E_DEV, dtype=jnp.int32)
    dest_sorted = jnp.sum((ends[:, :, None, :] <= events[None, None, :, None]).astype(jnp.int32), axis=3)
    slot_sorted = events[None, None, :] - jnp.take_along_axis(starts, dest_sorted, axis=2)
    order_keys = jax.random.split(key_order, N_REP * N_SHARD)
    orders = jax.vmap(lambda one: jax.random.permutation(one, E_DEV))(order_keys).reshape(N_REP, N_SHARD, E_DEV)
    dest_all = jnp.take_along_axis(dest_sorted, orders, axis=2).reshape(N_REP, N_SHARD * E_DEV)
    slot_all = jnp.take_along_axis(slot_sorted, orders, axis=2).reshape(N_REP, N_SHARD * E_DEV)
    within = jnp.arange(SLOT, dtype=jnp.int32)
    received = jnp.transpose(counts, (0, 2, 1))
    filled = within[None, None, None, :] < received[:, :, :, None]
    users = jax.random.randint(key_user, (N_REP, N_SHARD, N_SHARD, SLOT), 0, USERS).astype(jnp.int32)
    users = jnp.where(filled, users, -1).reshape(N_REP, N_SHARD * CAP)
    time_keys = jax.random.split(key_time, N_REP * N_SHARD)
    times = jax.vmap(lambda one: jax.random.permutation(one, CAP))(time_keys).reshape(N_REP, N_SHARD * CAP)
    return (dest_all.astype(jnp.int32), slot_all.astype(jnp.int32), users, times.astype(jnp.int32))


def draw_dest(key, part):
    return route_plan(key)[0]


def draw_slot(key, part):
    return route_plan(key)[1]


def draw_slot_user(key, part):
    return route_plan(key)[2]


def draw_slot_time(key, part):
    return route_plan(key)[3]


def block_scale(stream_key, dims, cuts, low, top_value):
    def one(position, blocks):
        heights = jax.random.uniform(jax.random.fold_in(jax.random.fold_in(stream_key, 6), position), (blocks,), jnp.float32, low / len(cuts), top_value / len(cuts))
        return jnp.repeat(jnp.exp(heights), dims[position] // blocks).reshape((-1,) + (1,) * (len(dims) - position - 1))

    gain = one(*cuts[0])
    for cut in cuts[1:]:
        gain = gain * one(*cut)
    return gain


def scatter_about(own_key, shape, spread, reach, cuts=(), kind=jnp.bfloat16):
    entries = spread * jax.random.normal(own_key, shape, jnp.float32)
    if cuts:
        entries = entries * block_scale(own_key, shape, cuts, -0.22, 0.18)
    return jnp.clip(entries, -reach, reach).astype(kind)


def setup_inputs(seed: int = 0) -> dict:
    key_list = jax.random.split(jax.random.key(seed), 9)
    inputs = scatter_about(key_list[0], (N_REP, GROUP_EVENTS, D), 1.0, 6.0, ((0, 8), (1, 4)))
    w_in = scatter_about(key_list[1], (D, 4 * D), D ** -0.5, 0.25)
    grad_out = scatter_about(key_list[2], (N_REP, GROUP_EVENTS, D), 1.0, 6.0, ((0, 8), (1, 4)))
    w_out = scatter_about(key_list[3], (D, D), D ** -0.5, 0.25)
    dest = draw_dest(jax.random.fold_in(key_list[8], 71), 0)
    slot = draw_slot(jax.random.fold_in(key_list[8], 71), 0)
    slot_user = draw_slot_user(jax.random.fold_in(key_list[8], 71), 0)
    slot_time = draw_slot_time(jax.random.fold_in(key_list[8], 71), 0)
    return dict(inputs=inputs, w_in=w_in, grad_out=grad_out, w_out=w_out, dest=dest, slot=slot, slot_user=slot_user, slot_time=slot_time)


def silu_slope(value):
    sig = jax.nn.sigmoid(value)
    return sig * (1.0 + value * (1.0 - sig))

def owner_pass(act, dy_rows, users, times, w_out):
    cap = act.shape[0]
    width = act.shape[1] // 4
    head_dim = width // HEADS
    scale = 1.0 / math.sqrt(head_dim)
    u_part = act[:, :width].astype(jnp.float32)
    v_heads = act[:, width:2 * width].astype(jnp.float32).reshape(cap, HEADS, head_dim)
    q_heads = act[:, 2 * width:3 * width].astype(jnp.float32).reshape(cap, HEADS, head_dim)
    k_heads = act[:, 3 * width:].astype(jnp.float32).reshape(cap, HEADS, head_dim)
    mask = (users[:, None] == users[None, :]) & (times[None, :] <= times[:, None]) & (users[:, None] >= 0)
    scores = jnp.einsum('ihd,jhd->hij', q_heads, k_heads) * scale
    sig = jax.nn.sigmoid(scores)
    attn = jnp.where(mask[None], scores * sig, 0.0).astype(jnp.bfloat16)
    attn_f = attn.astype(jnp.float32)
    out = jnp.einsum('hij,jhd->ihd', attn_f, v_heads).reshape(cap, width)
    centred = out - lax.optimization_barrier(jnp.mean(out, axis=1, keepdims=True))
    recip = lax.rsqrt(lax.optimization_barrier(jnp.mean(centred * centred, axis=1, keepdims=True)) + 1e-05)
    nrm = centred * recip
    zed = (nrm * u_part).astype(jnp.bfloat16)
    part_w = jnp.dot(zed.T, dy_rows, preferred_element_type=jnp.float32)
    dzed = jnp.dot(dy_rows, w_out.T, preferred_element_type=jnp.float32)
    grad_u = dzed * nrm
    grad_n = dzed * u_part
    grad_o = recip * (grad_n - lax.optimization_barrier(jnp.mean(grad_n, axis=1, keepdims=True)) - nrm * lax.optimization_barrier(jnp.mean(grad_n * nrm, axis=1, keepdims=True)))
    grad_o = grad_o.astype(jnp.bfloat16).astype(jnp.float32).reshape(cap, HEADS, head_dim)
    grad_a = jnp.einsum('ihd,jhd->hij', grad_o, v_heads)
    grad_v = jnp.einsum('hij,ihd->jhd', attn_f, grad_o)
    grad_s = jnp.where(mask[None], grad_a * sig * (1.0 + scores * (1.0 - sig)) * scale, 0.0)
    grad_s = grad_s.astype(jnp.bfloat16).astype(jnp.float32)
    grad_q = jnp.einsum('hij,jhd->ihd', grad_s, k_heads)
    grad_k = jnp.einsum('hij,ihd->jhd', grad_s, q_heads)
    grad_act = jnp.concatenate([grad_u, grad_v.reshape(cap, width), grad_q.reshape(cap, width), grad_k.reshape(cap, width)], axis=1).astype(jnp.bfloat16)
    return (lax.optimization_barrier(grad_act), part_w)

def reference(inputs, w_in, grad_out, w_out, dest, slot, slot_user, slot_time):

    def group(items):
        rows, dy_rows, dest_g, slot_g, users_g, times_g = items
        source = (jnp.arange(N_SHARD * E_DEV, dtype=jnp.int32) // E_DEV).astype(jnp.int32)
        flat = (dest_g * CAP + source * SLOT + slot_g).astype(jnp.int32)
        row_buf = jnp.zeros((N_SHARD * CAP, D), jnp.bfloat16).at[flat].set(rows).reshape(N_SHARD, CAP, D)
        dy_buf = jnp.zeros((N_SHARD * CAP, D), jnp.bfloat16).at[flat].set(dy_rows).reshape(N_SHARD, CAP, D)

        def owner(pieces):
            row_o, dy_o, users_o, times_o = pieces
            proj = jnp.dot(row_o, w_in, preferred_element_type=jnp.float32)
            act = (proj * jax.nn.sigmoid(proj)).astype(jnp.bfloat16)
            grad_act, part_w = owner_pass(act, dy_o, users_o, times_o, w_out)
            grad_h = (grad_act.astype(jnp.float32) * silu_slope(proj)).astype(jnp.bfloat16)
            return (grad_h, part_w)
        grad_all, parts = lax.map(owner, (row_buf, dy_buf, users_g.reshape(N_SHARD, CAP), times_g.reshape(N_SHARD, CAP)))
        grad_rows = grad_all.reshape(N_SHARD * CAP, 4 * D)[flat]
        return (grad_rows, lax.optimization_barrier(jnp.sum(parts, axis=0)))
    grads, parts = lax.map(group, (inputs, grad_out, dest, slot, slot_user, slot_time))
    total = lax.optimization_barrier(jnp.sum(parts, axis=0)) * (1.0 / math.sqrt(N_REP * N_SHARD * E_DEV))
    return (grads, total)
```

```python
import functools
import math

import jax
import jax.numpy as jnp
from jax import lax
from jax.experimental import pallas as pl
from jax.experimental.pallas import tpu as pltpu
from jax.sharding import PartitionSpec as P

HEADS = 4
F32 = jnp.float32
BF16 = jnp.bfloat16
TIMES = 512
USERS = 4
VMEM = pl.BlockSpec(memory_space=pltpu.VMEM)
SMEM = pl.BlockSpec(memory_space=pltpu.SMEM)


def silu_slope(value):
    sigma = jax.nn.sigmoid(value)
    return sigma * (1.0 + value * (1.0 - sigma))


def owner_pass(act, dy_rows, users, times, w_out):
    cap = act.shape[0]
    width = act.shape[1] // 4
    head_dim = width // HEADS
    scale = 1.0 / math.sqrt(head_dim)
    u_part = act[:, :width]
    v_heads = act[:, width : 2 * width].reshape(cap, HEADS, head_dim)
    q_heads = act[:, 2 * width : 3 * width].reshape(cap, HEADS, head_dim)
    k_heads = act[:, 3 * width :].reshape(cap, HEADS, head_dim)
    mask = (
        (users[:, None] == users[None, :])
        & (times[None, :] <= times[:, None])
        & (users[:, None] >= 0)
    )
    scores = (
        jnp.einsum("ihd,jhd->hij", q_heads, k_heads, preferred_element_type=jnp.float32) * scale
    )
    sigma = jax.nn.sigmoid(scores)
    attn = jnp.where(mask[None], scores * sigma, 0.0).astype(jnp.bfloat16)
    out = jnp.einsum("hij,jhd->ihd", attn, v_heads, preferred_element_type=jnp.float32).reshape(
        cap, width
    )
    centred = out - jnp.mean(out, axis=1, keepdims=True)
    recip = lax.rsqrt(jnp.mean(centred * centred, axis=1, keepdims=True) + 1e-05)
    nrm = centred * recip
    u_wide = u_part.astype(jnp.float32)
    zed = (nrm * u_wide).astype(jnp.bfloat16)
    part_w = lax.dot_general(
        zed, dy_rows, (((0,), (0,)), ((), ())), preferred_element_type=jnp.float32
    )
    dzed = lax.dot_general(
        dy_rows, w_out, (((1,), (1,)), ((), ())), preferred_element_type=jnp.float32
    )
    grad_u = dzed * nrm
    grad_n = dzed * u_wide
    grad_o = recip * (
        grad_n
        - jnp.mean(grad_n, axis=1, keepdims=True)
        - nrm * jnp.mean(grad_n * nrm, axis=1, keepdims=True)
    )
    grad_o = grad_o.astype(jnp.bfloat16).reshape(cap, HEADS, head_dim)
    grad_a = jnp.einsum("ihd,jhd->hij", grad_o, v_heads, preferred_element_type=jnp.float32)
    grad_v = jnp.einsum("hij,ihd->jhd", attn, grad_o, preferred_element_type=jnp.float32)
    grad_s = jnp.where(
        mask[None], grad_a * sigma * (1.0 + scores * (1.0 - sigma)) * scale, 0.0
    ).astype(jnp.bfloat16)
    grad_q = jnp.einsum("hij,jhd->ihd", grad_s, k_heads, preferred_element_type=jnp.float32)
    grad_k = jnp.einsum("hij,ihd->jhd", grad_s, q_heads, preferred_element_type=jnp.float32)
    grad_act = jnp.concatenate(
        [
            grad_u,
            grad_v.reshape(cap, width),
            grad_q.reshape(cap, width),
            grad_k.reshape(cap, width),
        ],
        axis=1,
    ).astype(jnp.bfloat16)
    return (lax.optimization_barrier(grad_act), part_w)


def routed(inputs, w_in, grad_out, w_out, dest, slot, slot_user, slot_time):
    shards = lax.axis_size("shard")
    groups = lax.axis_size("rep")
    per_dev = inputs.shape[1]
    width = inputs.shape[2]
    slots = 2 * per_dev // shards
    cap = shards * slots
    rows = inputs[0]
    flat = dest[0] * slots + slot[0]
    dy_buf = (
        jnp.zeros((cap, width), jnp.bfloat16)
        .at[flat]
        .set(grad_out[0])
        .reshape(shards, slots, width)
    )
    proj = jnp.dot(rows, w_in, preferred_element_type=jnp.float32)
    act = (proj * jax.nn.sigmoid(proj)).astype(jnp.bfloat16)
    act_buf = (
        jnp.zeros((cap, 4 * width), jnp.bfloat16)
        .at[flat]
        .set(act)
        .reshape(shards, slots, 4 * width)
    )
    got_act, got_dy = (
        lax.all_to_all(act_buf, "shard", split_axis=0, concat_axis=0, tiled=True),
        lax.all_to_all(dy_buf, "shard", split_axis=0, concat_axis=0, tiled=True),
    )
    owner_act = got_act.reshape(cap, 4 * width)
    grad_act, part_w = owner_pass(
        owner_act, got_dy.reshape(cap, width), slot_user[0], slot_time[0], w_out
    )
    back = lax.all_to_all(
        grad_act.reshape(shards, slots, 4 * width), "shard", split_axis=0, concat_axis=0, tiled=True
    )
    mine = back.reshape(cap, 4 * width)[flat]
    grad_rows = (mine.astype(jnp.float32) * silu_slope(proj)).astype(jnp.bfloat16)
    factor = 1.0 / math.sqrt(groups * shards * per_dev)
    summed = lax.psum(part_w, ("shard", "rep"))
    return (grad_rows[None], summed * factor)


def dot(a, b):
    return jnp.dot(a, b, preferred_element_type=F32)


def dot_nt(a, b):
    return lax.dot_general(a, b, (((1,), (1,)), ((), ())), preferred_element_type=F32)


def call(body, outs, specs, args, flops=0, moved=0, scratch=()):
    return pl.pallas_call(
        body,
        out_shape=outs,
        in_specs=specs,
        out_specs=jax.tree.map(lambda _: VMEM, outs),
        scratch_shapes=list(scratch),
        compiler_params=pltpu.CompilerParams(vmem_limit_bytes=24 << 20),
        cost_estimate=pl.CostEstimate(flops=flops, bytes_accessed=moved, transcendentals=0),
    )(*args)


def shaped(shape, kind):
    return jax.ShapeDtypeStruct(shape, kind)


def project(x, w_ref, first, last, step, put):
    for col in range(first, last, step):
        h = dot(x, w_ref[:, col : col + step])
        put(col, h)


def project_own_body(x_ref, w_ref, u_ref, vqk_ref, slope_ref):
    width = u_ref.shape[1]
    x = x_ref[...]

    def put(col, h):
        half = 0.5 * h
        t = jnp.tanh(half)
        act = half + half * t
        slope_ref[:, col : col + 256] = 0.5 * ((1.0 + t) + act * (1.0 - t))
        out = act.astype(BF16)
        if col < width:
            u_ref[:, col : col + 256] = out
        else:
            vqk_ref[:, col - width : col - width + 256] = out

    project(x, w_ref, 0, 4 * width, 256, put)


def project_body(x_ref, w_ref, *out_refs):
    vqk_ref = out_refs[-1]
    width = vqk_ref.shape[1] // 3
    x = x_ref[...]

    def put(col, h):
        half = 0.5 * h
        act = (half + half * jnp.tanh(half)).astype(BF16)
        if col < width:
            out_refs[0][:, col : col + 256] = act
        else:
            vqk_ref[:, col - width : col - width + 256] = act

    project(x, w_ref, 0 if len(out_refs) == 2 else width, 4 * width, 256, put)


def codes_body(place_ref, i0, i1, i2, i3, lane_ref, sub_ref):
    infos = (i0, i1, i2, i3)
    me = place_ref[0]
    ids = (me, me ^ 2, me ^ 1, me ^ 3)
    events = lane_ref.shape[1]
    slots = events // 2
    row8 = lax.broadcasted_iota(jnp.int32, (8, slots), 0)
    down = lax.broadcasted_iota(jnp.int32, (slots, events), 0)
    rows = []
    for b in range(4):
        flat = infos[b][:, 0:events] * slots + infos[b][:, events : 2 * events]
        total = jnp.zeros((8, events), F32)
        for p in range(4):
            at = pl.multiple_of(2 * events + ids[b] * slots, slots)
            user = infos[p][:, pl.ds(at, slots)]
            at = pl.multiple_of(4 * events + ids[b] * slots, slots)
            when = infos[p][:, pl.ds(at, slots)]
            who = ids[p] * USERS + user
            table = jnp.where(
                row8 == 0, who, jnp.where(row8 == 1, when >> 8, jnp.where(row8 == 2, when & 255, 0))
            )
            hit = (down + ids[p] * slots) == flat
            total += dot(
                table.astype(F32).astype(BF16), jnp.where(hit, 1.0, 0.0).astype(BF16)
            )
        rows.append(total[0:1] * TIMES + total[1:2] * 256.0 + total[2:3])
    codes = jnp.concatenate(rows + rows, axis=0)
    lane_ref[...] = codes
    sub_ref[...] = codes.T


def pair_mask(low, high, key):
    return jnp.where((key >= low) & (key <= high), 1.0, 0.0).astype(BF16)


def attend(head, q_ref, kv_refs, masks, half_scale):
    width = q_ref.shape[1] // 3
    dim = width // HEADS
    at = head * dim
    q = q_ref[:, width + at : width + at + dim]
    total = None
    for kv_ref, mask in zip(kv_refs, masks):
        half = dot_nt(q, kv_ref[:, 2 * width + at : 2 * width + at + dim]) * half_scale
        attn = (half + half * jnp.tanh(half)).astype(BF16) * mask
        part = dot(attn, kv_ref[:, at : at + dim])
        total = part if total is None else total + part
    return total


def normed(out):
    centred = out - jnp.mean(out, axis=1, keepdims=True)
    recip = lax.rsqrt(jnp.mean(centred * centred, axis=1, keepdims=True) + 1e-05)
    return centred * recip, recip


def row_masks(sub_ref, lane_ref, column):
    high = sub_ref[:, column : column + 1]
    low = jnp.floor(high * (1.0 / TIMES)) * TIMES
    return [pair_mask(low, high, lane_ref[b : b + 1, :]) for b in range(4)]


def forward_body(
    half_scale, place_ref, v0, v1, v2, v3, u_ref, lane_ref, sub_ref, dy_ref,
    mine_ref, other_ref, nrm_ref, recip_ref, o_ref, zt_ref,
):
    kv_refs = (v0, v1, v2, v3)
    dim = u_ref.shape[1] // HEADS
    masks = row_masks(sub_ref, lane_ref, 0)
    for head in range(HEADS):
        o_ref[:, head * dim : (head + 1) * dim] = attend(head, v0, kv_refs, masks, half_scale)
    nrm, recip = normed(o_ref[...])
    nrm_ref[...] = nrm
    recip_ref[...] = jnp.broadcast_to(recip, recip_ref.shape)
    zt_ref[...] = (nrm * u_ref[...].astype(F32)).T.astype(BF16)
    rows = mine_ref.shape[0]
    core = place_ref[1]
    dy = dy_ref[...]
    other_ref[...] = dot(zt_ref[pl.ds(pl.multiple_of((1 - core) * rows, rows), rows), :], dy).astype(BF16)
    mine_ref[...] = dot(zt_ref[pl.ds(pl.multiple_of(core * rows, rows), rows), :], dy)


def grad_o_of(dzed, u, nrm, recip):
    grad_n = dzed * u
    return (
        recip
        * (
            grad_n
            - jnp.mean(grad_n, axis=1, keepdims=True)
            - nrm * jnp.mean(grad_n * nrm, axis=1, keepdims=True)
        )
    ).astype(BF16)


def grad_o_body(
    half_scale, v0, v1, v2, v3, u0_ref, u1_ref, lane_ref, sub_ref, dy0_ref, dy1_ref, w_out_ref,
    nrm_ref, recip_ref, slope_ref, do_ref, gu_ref, o_ref,
):
    kv_refs = (v0, v1, v2, v3)
    rows, width = u0_ref.shape
    dim = width // HEADS
    w_out = w_out_ref[...]
    dzed = dot_nt(dy0_ref[...], w_out)
    nrm = nrm_ref[...]
    gu_ref[...] = ((dzed * nrm).astype(BF16).astype(F32) * slope_ref[:, :width]).astype(BF16)
    do_ref[0:rows, :] = grad_o_of(dzed, u0_ref[...].astype(F32), nrm, recip_ref[:, 0:1])
    masks = row_masks(sub_ref, lane_ref, 1)
    for head in range(HEADS):
        o_ref[:, head * dim : (head + 1) * dim] = attend(head, v1, kv_refs, masks, half_scale)
    nrm, recip = normed(o_ref[...])
    dzed = dot_nt(dy1_ref[...], w_out)
    do_ref[rows:, :] = grad_o_of(dzed, u1_ref[...].astype(F32), nrm, recip)


def grad_q_body(half_scale, v0, v1, v2, v3, lane_ref, sub_ref, do_ref, slope_ref, gq_ref):
    kv_refs = (v0, v1, v2, v3)
    rows, width = gq_ref.shape
    dim = width // HEADS
    masks = row_masks(sub_ref, lane_ref, 0)
    for head in range(HEADS):
        at = head * dim
        q = v0[:, width + at : width + at + dim]
        do = do_ref[0:rows, at : at + dim]
        total = None
        for kv_ref, mask in zip(kv_refs, masks):
            k = kv_ref[:, 2 * width + at : 2 * width + at + dim]
            half = dot_nt(q, k) * half_scale
            t = jnp.tanh(half)
            slope = (1.0 + t) + (half + half * t) * (1.0 - t)
            grad_s = (dot_nt(do, kv_ref[:, at : at + dim]) * slope).astype(BF16) * mask
            part = dot(grad_s, k)
            total = part if total is None else total + part
        grad = (total * half_scale).astype(BF16).astype(F32)
        gq_ref[:, at : at + dim] = (grad * slope_ref[:, 2 * width + at : 2 * width + at + dim]).astype(BF16)


def grad_kv_body(half_scale, v0, v1, v2, v3, lane_ref, sub_ref, do01_ref, do23_ref, slope_ref, gu_ref, gq_ref, out_ref):
    q_refs = (v0, v1, v2, v3)
    rows, width = gq_ref.shape
    dim = width // HEADS
    key = sub_ref[:, 0:1]
    masks = []
    for b in range(4):
        high = lane_ref[b : b + 1, :]
        low = jnp.floor(high * (1.0 / TIMES)) * TIMES
        masks.append(pair_mask(low, high, key))
    out_ref[0, :, 0:width] = gu_ref[...]
    out_ref[0, :, 2 * width : 3 * width] = gq_ref[...]
    for head in range(HEADS):
        at = head * dim
        v = v0[:, at : at + dim]
        k = v0[:, 2 * width + at : 2 * width + at + dim]
        sum_v = sum_k = None
        for b in range(4):
            q = q_refs[b][:, width + at : width + at + dim]
            do_ref = (do01_ref, do23_ref)[b // 2]
            do = do_ref[(b % 2) * rows : (b % 2 + 1) * rows, at : at + dim]
            half = dot_nt(k, q) * half_scale
            t = jnp.tanh(half)
            act = half + half * t
            slope = (1.0 + t) + act * (1.0 - t)
            part_v = dot(act.astype(BF16) * masks[b], do)
            grad_s = (dot_nt(v, do) * slope).astype(BF16) * masks[b]
            part_k = dot(grad_s, q)
            sum_v = part_v if sum_v is None else sum_v + part_v
            sum_k = part_k if sum_k is None else sum_k + part_k
        for first, grad in ((width + at, sum_v), (3 * width + at, sum_k * half_scale)):
            grad = grad.astype(BF16).astype(F32)
            out_ref[0, :, first : first + dim] = (grad * slope_ref[:, first : first + dim]).astype(BF16)


def cut_body(place_ref, mine_ref, got_ref, own_ref, p1_ref, p2_ref, p3_ref, sum_ref):
    rows = own_ref.shape[0]
    z = place_ref[2]
    sum_ref[...] = mine_ref[...] + got_ref[...].astype(F32)
    own_ref[...] = sum_ref[pl.ds(pl.multiple_of(z * rows, rows), rows), :]
    for k, ref in ((1, p1_ref), (2, p2_ref), (3, p3_ref)):
        ref[...] = sum_ref[pl.ds(pl.multiple_of((z ^ k) * rows, rows), rows), :].astype(BF16)


def add_body(own_ref, r1, r2, r3, out_ref):
    out_ref[...] = (
        (own_ref[...].astype(F32) + r1[...].astype(F32)) + (r2[...].astype(F32) + r3[...].astype(F32))
    ).astype(BF16)


def join_body(place_ref, own_ref, r1, r2, r3, out_ref):
    rows = own_ref.shape[0]
    z = place_ref[2]
    for k, ref in enumerate((own_ref, r1, r2, r3)):
        out_ref[pl.ds(pl.multiple_of((z ^ k) * rows, rows), rows), :] = ref[...]


def final_body(factor, place_ref, own_ref, got_ref, out_ref):
    rows = own_ref.shape[0]
    core = place_ref[1]
    out_ref[pl.ds(pl.multiple_of(core * rows, rows), rows), :] = own_ref[...].astype(F32) * factor
    out_ref[pl.ds(pl.multiple_of((1 - core) * rows, rows), rows), :] = got_ref[...].astype(F32) * factor


def swap(value, shard_bits, rep_bits=0):
    pairs = [(i, i ^ (shard_bits * 8 + rep_bits)) for i in range(32)]
    return lax.ppermute(value, ("shard", "rep"), pairs)


def by_event(inputs, w_in, grad_out, w_out, dest, slot, slot_user, slot_time):
    x, dy = inputs[0], grad_out[0]
    events, width = x.shape
    half_scale = 0.5 / math.sqrt(width // HEADS)
    factor = 1.0 / math.sqrt(32 * events)
    me, rep = lax.axis_index("shard"), lax.axis_index("rep")
    place = jnp.stack([me, me % 2, rep // 2, rep % 2]).astype(jnp.int32)
    vqk = shaped((events, 3 * width), BF16)
    square = shaped((events, width), BF16)
    wide = 2 * events * width

    x_y = swap(x, 2)
    info = jnp.concatenate([dest, slot, slot_user, slot_time], axis=1)
    info_y = swap(info, 2)
    x_c = swap(x, 1)
    info_c = swap(info, 1)
    u_o, vqk_o, slope = call(
        project_own_body, [square, vqk, shaped((events, 4 * width), F32)], [VMEM] * 2, (x, w_in),
        flops=wide * 4 * width, moved=6 << 20,
    )
    (vqk_c,) = call(project_body, [vqk], [VMEM] * 2, (x_c, w_in), flops=wide * 3 * width, moved=3 << 20)
    info_d = swap(info_y, 1)
    lane, sub = call(
        codes_body, [shaped((8, events), F32), shaped((events, 8), F32)], [SMEM] + [VMEM] * 4,
        (place, info, info_y, info_c, info_d), flops=1 << 28, moved=1 << 20,
    )
    x_d = swap(x_y, 1)
    u_y, vqk_y = call(project_body, [square, vqk], [VMEM] * 2, (x_y, w_in), flops=wide * 4 * width, moved=3 << 20)
    (vqk_d,) = call(project_body, [vqk], [VMEM] * 2, (x_d, w_in), flops=wide * 3 * width, moved=3 << 20)
    kv = (vqk_o, vqk_y, vqk_c, vqk_d)

    half = shaped((width // 2, width), F32)
    mine, other, nrm, recip = call(
        functools.partial(forward_body, half_scale),
        [half, shaped(half.shape, BF16), shaped((events, width), F32), shaped((events, 128), F32)],
        [SMEM] + [VMEM] * 8,
        (place, *kv, u_o, lane, sub, dy),
        flops=wide * 4 * events * 3, moved=6 << 20,
        scratch=[pltpu.VMEM((events, width), F32), pltpu.VMEM((width, events), BF16)],
    )
    got = swap(other, 1)
    dy, _ = lax.optimization_barrier((dy, other))
    dy_y = swap(dy, 2)
    block = shaped((width // 8, width), BF16)
    own, p1, p2, p3 = call(
        cut_body, [shaped(block.shape, F32), block, block, block], [SMEM] + [VMEM] * 2, (place, mine, got),
        flops=1 << 20, moved=1 << 20, scratch=[pltpu.VMEM(half.shape, F32)],
    )
    r1, r2, r3 = swap(p1, 0, 2), swap(p2, 0, 4), swap(p3, 0, 6)
    do_oy, gu = call(
        functools.partial(grad_o_body, half_scale),
        [shaped((2 * events, width), BF16), square], [VMEM] * 14,
        (*kv, u_o, u_y, lane, sub, dy, dy_y, w_out, nrm, recip, slope),
        flops=wide * 4 * events * 4, moved=8 << 20,
        scratch=[pltpu.VMEM((events, width), F32)],
    )
    do_cd = swap(do_oy, 1)
    (part,) = call(add_body, [block], [VMEM] * 4, (own, r1, r2, r3), flops=1 << 18, moved=1 << 19)
    r1, r2, r3 = swap(part, 0, 1), swap(part, 2, 0), swap(part, 2, 1)
    (gq,) = call(
        functools.partial(grad_q_body, half_scale), [square], [VMEM] * 8,
        (*kv, lane, sub, do_oy, slope), flops=wide * 4 * events * 4, moved=6 << 20,
    )
    (part,) = call(add_body, [block], [VMEM] * 4, (part, r1, r2, r3), flops=1 << 18, moved=1 << 19)
    r1, r2, r3 = swap(part, 0, 2), swap(part, 0, 4), swap(part, 0, 6)
    (grad_rows,) = call(
        functools.partial(grad_kv_body, half_scale), [shaped((1, events, 4 * width), BF16)], [VMEM] * 11,
        (*kv, lane, sub, do_oy, do_cd, slope, gu, gq), flops=wide * 4 * events * 6, moved=8 << 20,
    )
    (mine,) = call(
        join_body, [shaped(half.shape, BF16)], [SMEM] + [VMEM] * 4, (place, part, r1, r2, r3),
        flops=1 << 18, moved=1 << 19,
    )
    got = swap(mine, 1)
    (grad_w,) = call(
        functools.partial(final_body, factor), [shaped((width, width), F32)], [SMEM] + [VMEM] * 2,
        (place, mine, got), flops=1 << 18, moved=2 << 20,
    )
    return grad_rows, grad_w


def on_device(*args):
    events, width = args[0].shape[1:]
    plain = lax.axis_size("shard") == 4 and lax.axis_size("rep") == 8
    if plain and events == 256 and width == 512:
        return by_event(*args)
    return routed(*args)


def solution(mesh):
    return jax.shard_map(
        on_device,
        mesh=mesh,
        in_specs=(
            P("rep", "shard", None),
            P(),
            P("rep", "shard", None),
            P(),
            P("rep", "shard"),
            P("rep", "shard"),
            P("rep", "shard"),
            P("rep", "shard"),
        ),
        out_specs=(P("rep", "shard", None), P()),
        check_vma=False,
    )
```

```python
import functools
import math

import jax
import jax.numpy as jnp
from jax import lax
from jax.experimental import pallas as pl
from jax.experimental.pallas import tpu as pltpu
from jax.sharding import PartitionSpec as P

HEADS = 4
F32 = jnp.float32
BF16 = jnp.bfloat16
TIMES = 512
USERS = 4
VMEM = pl.BlockSpec(memory_space=pltpu.VMEM)
SMEM = pl.BlockSpec(memory_space=pltpu.SMEM)
HBM = pl.BlockSpec(memory_space=pltpu.HBM)


def silu_slope(value):
    sigma = jax.nn.sigmoid(value)
    return sigma * (1.0 + value * (1.0 - sigma))


def owner_pass(act, dy_rows, users, times, w_out):
    cap = act.shape[0]
    width = act.shape[1] // 4
    head_dim = width // HEADS
    scale = 1.0 / math.sqrt(head_dim)
    u_part = act[:, :width]
    v_heads = act[:, width : 2 * width].reshape(cap, HEADS, head_dim)
    q_heads = act[:, 2 * width : 3 * width].reshape(cap, HEADS, head_dim)
    k_heads = act[:, 3 * width :].reshape(cap, HEADS, head_dim)
    mask = (
        (users[:, None] == users[None, :])
        & (times[None, :] <= times[:, None])
        & (users[:, None] >= 0)
    )
    scores = (
        jnp.einsum("ihd,jhd->hij", q_heads, k_heads, preferred_element_type=jnp.float32) * scale
    )
    sigma = jax.nn.sigmoid(scores)
    attn = jnp.where(mask[None], scores * sigma, 0.0).astype(jnp.bfloat16)
    out = jnp.einsum("hij,jhd->ihd", attn, v_heads, preferred_element_type=jnp.float32).reshape(
        cap, width
    )
    centred = out - jnp.mean(out, axis=1, keepdims=True)
    recip = lax.rsqrt(jnp.mean(centred * centred, axis=1, keepdims=True) + 1e-05)
    nrm = centred * recip
    u_wide = u_part.astype(jnp.float32)
    zed = (nrm * u_wide).astype(jnp.bfloat16)
    part_w = lax.dot_general(
        zed, dy_rows, (((0,), (0,)), ((), ())), preferred_element_type=jnp.float32
    )
    dzed = lax.dot_general(
        dy_rows, w_out, (((1,), (1,)), ((), ())), preferred_element_type=jnp.float32
    )
    grad_u = dzed * nrm
    grad_n = dzed * u_wide
    grad_o = recip * (
        grad_n
        - jnp.mean(grad_n, axis=1, keepdims=True)
        - nrm * jnp.mean(grad_n * nrm, axis=1, keepdims=True)
    )
    grad_o = grad_o.astype(jnp.bfloat16).reshape(cap, HEADS, head_dim)
    grad_a = jnp.einsum("ihd,jhd->hij", grad_o, v_heads, preferred_element_type=jnp.float32)
    grad_v = jnp.einsum("hij,ihd->jhd", attn, grad_o, preferred_element_type=jnp.float32)
    grad_s = jnp.where(
        mask[None], grad_a * sigma * (1.0 + scores * (1.0 - sigma)) * scale, 0.0
    ).astype(jnp.bfloat16)
    grad_q = jnp.einsum("hij,jhd->ihd", grad_s, k_heads, preferred_element_type=jnp.float32)
    grad_k = jnp.einsum("hij,ihd->jhd", grad_s, q_heads, preferred_element_type=jnp.float32)
    grad_act = jnp.concatenate(
        [
            grad_u,
            grad_v.reshape(cap, width),
            grad_q.reshape(cap, width),
            grad_k.reshape(cap, width),
        ],
        axis=1,
    ).astype(jnp.bfloat16)
    return (lax.optimization_barrier(grad_act), part_w)


def routed(inputs, w_in, grad_out, w_out, dest, slot, slot_user, slot_time):
    shards = lax.axis_size("shard")
    groups = lax.axis_size("rep")
    per_dev = inputs.shape[1]
    width = inputs.shape[2]
    slots = 2 * per_dev // shards
    cap = shards * slots
    rows = inputs[0]
    flat = dest[0] * slots + slot[0]
    dy_buf = (
        jnp.zeros((cap, width), jnp.bfloat16)
        .at[flat]
        .set(grad_out[0])
        .reshape(shards, slots, width)
    )
    proj = jnp.dot(rows, w_in, preferred_element_type=jnp.float32)
    act = (proj * jax.nn.sigmoid(proj)).astype(jnp.bfloat16)
    act_buf = (
        jnp.zeros((cap, 4 * width), jnp.bfloat16)
        .at[flat]
        .set(act)
        .reshape(shards, slots, 4 * width)
    )
    got_act, got_dy = (
        lax.all_to_all(act_buf, "shard", split_axis=0, concat_axis=0, tiled=True),
        lax.all_to_all(dy_buf, "shard", split_axis=0, concat_axis=0, tiled=True),
    )
    owner_act = got_act.reshape(cap, 4 * width)
    grad_act, part_w = owner_pass(
        owner_act, got_dy.reshape(cap, width), slot_user[0], slot_time[0], w_out
    )
    back = lax.all_to_all(
        grad_act.reshape(shards, slots, 4 * width), "shard", split_axis=0, concat_axis=0, tiled=True
    )
    mine = back.reshape(cap, 4 * width)[flat]
    grad_rows = (mine.astype(jnp.float32) * silu_slope(proj)).astype(jnp.bfloat16)
    factor = 1.0 / math.sqrt(groups * shards * per_dev)
    summed = lax.psum(part_w, ("shard", "rep"))
    return (grad_rows[None], summed * factor)


def dot(a, b):
    return jnp.dot(a, b, preferred_element_type=F32)


def dot_nt(a, b):
    return lax.dot_general(a, b, (((1,), (1,)), ((), ())), preferred_element_type=F32)


def call(body, outs, specs, args, flops=0, moved=0, scratch=(), after=()):
    if after:
        last, *_ = lax.optimization_barrier((args[-1], *after))
        args = (*args[:-1], last)
    return pl.pallas_call(
        body,
        out_shape=outs,
        in_specs=specs,
        out_specs=jax.tree.map(lambda _: VMEM, outs),
        scratch_shapes=list(scratch),
        compiler_params=pltpu.CompilerParams(vmem_limit_bytes=16 << 20),
        cost_estimate=pl.CostEstimate(flops=flops, bytes_accessed=moved, transcendentals=0),
    )(*args)


def shaped(shape, kind):
    return jax.ShapeDtypeStruct(shape, kind)


def project(x, w_ref, first, last, step, put):
    for col in range(first, last, step):
        h = dot(x, w_ref[:, col : col + step])
        put(col, h)


def project_own_body(w_hbm, x_hbm, w_ref, u_ref, vqk_ref, slope_ref, x_ref, sem):
    width = u_ref.shape[1]
    copies = [pltpu.make_async_copy(x_hbm, x_ref, sem.at[4])]
    for i in range(4):
        block = pl.ds(i * width, width)
        copies.append(pltpu.make_async_copy(w_hbm.at[:, block], w_ref.at[:, block], sem.at[i]))
    for copy in copies:
        copy.start()
    copies[0].wait()
    x = x_ref[...]

    def put(col, h):
        half = 0.5 * h
        t = jnp.tanh(half)
        act = half + half * t
        slope_ref[:, col : col + 256] = 0.5 * ((1.0 + t) + act * (1.0 - t))
        out = act.astype(BF16)
        if col < width:
            u_ref[:, col : col + 256] = out
        else:
            vqk_ref[:, col - width : col - width + 256] = out

    for i in range(4):
        copies[i + 1].wait()
        project(x, w_ref, i * width, (i + 1) * width, 256, put)


def project_body(x_ref, w_ref, *out_refs):
    vqk_ref = out_refs[-1]
    width = vqk_ref.shape[1] // 3
    x = x_ref[...]

    def put(col, h):
        half = 0.5 * h
        act = (half + half * jnp.tanh(half)).astype(BF16)
        if col < width:
            out_refs[0][:, col : col + 256] = act
        else:
            vqk_ref[:, col - width : col - width + 256] = act

    project(x, w_ref, 0 if len(out_refs) == 2 else width, 4 * width, 256, put)


def pack_body(dest_ref, slot_ref, user_ref, time_ref, out_ref, sem):
    first, copies = 0, []
    for i, ref in enumerate((dest_ref, slot_ref, user_ref, time_ref)):
        copies.append(pltpu.make_async_copy(ref, out_ref.at[:, first : first + ref.shape[1]], sem.at[i]))
        first += ref.shape[1]
    for copy in copies:
        copy.start()
    for copy in copies:
        copy.wait()


def codes_body(place_ref, i0, i1, i2, i3, lane_ref, sub_ref):
    infos = (i0, i1, i2, i3)
    me = place_ref[0]
    ids = (me, me ^ 2, me ^ 1, me ^ 3)
    events = lane_ref.shape[1]
    slots = events // 2
    row8 = lax.broadcasted_iota(jnp.int32, (8, slots), 0)
    down = lax.broadcasted_iota(jnp.int32, (slots, events), 0)
    rows = []
    for b in range(4):
        flat = infos[b][:, 0:events] * slots + infos[b][:, events : 2 * events]
        total = jnp.zeros((8, events), F32)
        for p in range(4):
            at = pl.multiple_of(2 * events + ids[b] * slots, slots)
            user = infos[p][:, pl.ds(at, slots)]
            at = pl.multiple_of(4 * events + ids[b] * slots, slots)
            when = infos[p][:, pl.ds(at, slots)]
            who = ids[p] * USERS + user
            table = jnp.where(
                row8 == 0, who, jnp.where(row8 == 1, when >> 8, jnp.where(row8 == 2, when & 255, 0))
            )
            hit = (down + ids[p] * slots) == flat
            total += dot(
                table.astype(F32).astype(BF16), jnp.where(hit, 1.0, 0.0).astype(BF16)
            )
        rows.append(total[0:1] * TIMES + total[1:2] * 256.0 + total[2:3])
    codes = jnp.concatenate(rows + rows, axis=0)
    lane_ref[...] = codes
    sub_ref[...] = codes.T


def pair_mask(low, high, key):
    return jnp.where((key >= low) & (key <= high), 1.0, 0.0).astype(BF16)


def attend(head, q_ref, kv_refs, masks, half_scale):
    width = q_ref.shape[1] // 3
    dim = width // HEADS
    at = head * dim
    q = q_ref[:, width + at : width + at + dim]
    total = None
    for kv_ref, mask in zip(kv_refs, masks):
        half = dot_nt(q, kv_ref[:, 2 * width + at : 2 * width + at + dim]) * half_scale
        attn = (half + half * jnp.tanh(half)).astype(BF16) * mask
        part = dot(attn, kv_ref[:, at : at + dim])
        total = part if total is None else total + part
    return total


def normed(out):
    centred = out - jnp.mean(out, axis=1, keepdims=True)
    recip = lax.rsqrt(jnp.mean(centred * centred, axis=1, keepdims=True) + 1e-05)
    return centred * recip, recip


def row_masks(sub_ref, lane_ref, column):
    high = sub_ref[:, column : column + 1]
    low = jnp.floor(high * (1.0 / TIMES)) * TIMES
    return [pair_mask(low, high, lane_ref[b : b + 1, :]) for b in range(4)]


def forward_body(
    half_scale, place_ref, v0, v1, v2, v3, u_ref, lane_ref, sub_ref, dy_ref,
    mine_ref, other_ref, nrm_ref, recip_ref, o_ref, zt_ref,
):
    kv_refs = (v0, v1, v2, v3)
    dim = u_ref.shape[1] // HEADS
    masks = row_masks(sub_ref, lane_ref, 0)
    for head in range(HEADS):
        o_ref[:, head * dim : (head + 1) * dim] = attend(head, v0, kv_refs, masks, half_scale)
    nrm, recip = normed(o_ref[...])
    nrm_ref[...] = nrm
    recip_ref[...] = jnp.broadcast_to(recip, recip_ref.shape)
    zt_ref[...] = (nrm * u_ref[...].astype(F32)).T.astype(BF16)
    rows = mine_ref.shape[0]
    core = place_ref[1]
    dy = dy_ref[...]
    other_ref[...] = dot(zt_ref[pl.ds(pl.multiple_of((1 - core) * rows, rows), rows), :], dy).astype(BF16)
    mine_ref[...] = dot(zt_ref[pl.ds(pl.multiple_of(core * rows, rows), rows), :], dy)


def grad_o_of(dzed, u, nrm, recip):
    grad_n = dzed * u
    return (
        recip
        * (
            grad_n
            - jnp.mean(grad_n, axis=1, keepdims=True)
            - nrm * jnp.mean(grad_n * nrm, axis=1, keepdims=True)
        )
    ).astype(BF16)


def partner_body(half_scale, v0, v1, v2, v3, lane_ref, sub_ref, nrm_ref, recip_ref, o_ref):
    kv_refs = (v0, v1, v2, v3)
    dim = nrm_ref.shape[1] // HEADS
    masks = row_masks(sub_ref, lane_ref, 1)
    for head in range(HEADS):
        o_ref[:, head * dim : (head + 1) * dim] = attend(head, v1, kv_refs, masks, half_scale)
    nrm, recip = normed(o_ref[...])
    nrm_ref[...] = nrm
    recip_ref[...] = jnp.broadcast_to(recip, recip_ref.shape)


def grad_o_body(
    u0_ref, u1_ref, dy0_ref, dy1_ref, w_out_ref, nrm0_ref, recip0_ref, nrm1_ref, recip1_ref, slope_ref,
    do_ref, gu_ref,
):
    rows, width = u0_ref.shape
    w_out = w_out_ref[...]
    dzed = dot_nt(dy0_ref[...], w_out)
    nrm = nrm0_ref[...]
    gu_ref[...] = ((dzed * nrm).astype(BF16).astype(F32) * slope_ref[:, :width]).astype(BF16)
    do_ref[0:rows, :] = grad_o_of(dzed, u0_ref[...].astype(F32), nrm, recip0_ref[:, 0:1])
    dzed = dot_nt(dy1_ref[...], w_out)
    do_ref[rows:, :] = grad_o_of(dzed, u1_ref[...].astype(F32), nrm1_ref[...], recip1_ref[:, 0:1])


def grad_q_body(half_scale, v0, v1, v2, v3, lane_ref, sub_ref, do_ref, slope_ref, gq_ref):
    kv_refs = (v0, v1, v2, v3)
    rows, width = gq_ref.shape
    dim = width // HEADS
    masks = row_masks(sub_ref, lane_ref, 0)
    for head in range(HEADS):
        at = head * dim
        q = v0[:, width + at : width + at + dim]
        do = do_ref[0:rows, at : at + dim]
        total = None
        for kv_ref, mask in zip(kv_refs, masks):
            k = kv_ref[:, 2 * width + at : 2 * width + at + dim]
            half = dot_nt(q, k) * half_scale
            t = jnp.tanh(half)
            slope = (1.0 + t) + (half + half * t) * (1.0 - t)
            grad_s = (dot_nt(do, kv_ref[:, at : at + dim]) * slope).astype(BF16) * mask
            part = dot(grad_s, k)
            total = part if total is None else total + part
        grad = (total * half_scale).astype(BF16).astype(F32)
        gq_ref[:, at : at + dim] = (grad * slope_ref[:, 2 * width + at : 2 * width + at + dim]).astype(BF16)


def grad_kv_body(half_scale, v0, v1, v2, v3, lane_ref, sub_ref, do01_ref, do23_ref, slope_ref, gu_ref, gq_ref, out_ref):
    q_refs = (v0, v1, v2, v3)
    rows, width = gq_ref.shape
    dim = width // HEADS
    key = sub_ref[:, 0:1]
    masks = []
    for b in range(4):
        high = lane_ref[b : b + 1, :]
        low = jnp.floor(high * (1.0 / TIMES)) * TIMES
        masks.append(pair_mask(low, high, key))
    out_ref[0, :, 0:width] = gu_ref[...]
    out_ref[0, :, 2 * width : 3 * width] = gq_ref[...]
    for head in range(HEADS):
        at = head * dim
        v = v0[:, at : at + dim]
        k = v0[:, 2 * width + at : 2 * width + at + dim]
        sum_v = sum_k = None
        for b in range(4):
            q = q_refs[b][:, width + at : width + at + dim]
            do_ref = (do01_ref, do23_ref)[b // 2]
            do = do_ref[(b % 2) * rows : (b % 2 + 1) * rows, at : at + dim]
            half = dot_nt(k, q) * half_scale
            t = jnp.tanh(half)
            act = half + half * t
            slope = (1.0 + t) + act * (1.0 - t)
            part_v = dot(act.astype(BF16) * masks[b], do)
            grad_s = (dot_nt(v, do) * slope).astype(BF16) * masks[b]
            part_k = dot(grad_s, q)
            sum_v = part_v if sum_v is None else sum_v + part_v
            sum_k = part_k if sum_k is None else sum_k + part_k
        for first, grad in ((width + at, sum_v), (3 * width + at, sum_k * half_scale)):
            grad = grad.astype(BF16).astype(F32)
            out_ref[0, :, first : first + dim] = (grad * slope_ref[:, first : first + dim]).astype(BF16)


def cut_body(place_ref, mine_ref, got_ref, own_ref, p1_ref, p2_ref, p3_ref, sum_ref):
    rows = own_ref.shape[0]
    z = place_ref[2]
    sum_ref[...] = mine_ref[...] + got_ref[...].astype(F32)
    own_ref[...] = sum_ref[pl.ds(pl.multiple_of(z * rows, rows), rows), :]
    for k, ref in ((1, p1_ref), (2, p2_ref), (3, p3_ref)):
        ref[...] = sum_ref[pl.ds(pl.multiple_of((z ^ k) * rows, rows), rows), :].astype(BF16)


def add_body(own_ref, r1, r2, r3, out_ref):
    out_ref[...] = (
        (own_ref[...].astype(F32) + r1[...].astype(F32)) + (r2[...].astype(F32) + r3[...].astype(F32))
    ).astype(BF16)


def join_body(place_ref, own_ref, r1, r2, r3, out_ref):
    rows = own_ref.shape[0]
    z = place_ref[2]
    for k, ref in enumerate((own_ref, r1, r2, r3)):
        out_ref[pl.ds(pl.multiple_of((z ^ k) * rows, rows), rows), :] = ref[...]


def final_body(factor, place_ref, own_ref, got_ref, out_ref):
    rows = own_ref.shape[0]
    core = place_ref[1]
    out_ref[pl.ds(pl.multiple_of(core * rows, rows), rows), :] = own_ref[...].astype(F32) * factor
    out_ref[pl.ds(pl.multiple_of((1 - core) * rows, rows), rows), :] = got_ref[...].astype(F32) * factor


def swap(value, shard_bits, rep_bits=0):
    pairs = [(i, i ^ (shard_bits * 8 + rep_bits)) for i in range(32)]
    return lax.ppermute(value, ("shard", "rep"), pairs)


def by_event(inputs, w_in, grad_out, w_out, dest, slot, slot_user, slot_time):
    x, dy = inputs[0], grad_out[0]
    events, width = x.shape
    half_scale = 0.5 / math.sqrt(width // HEADS)
    factor = 1.0 / math.sqrt(32 * events)
    me, rep = lax.axis_index("shard"), lax.axis_index("rep")
    place = jnp.stack([me, me % 2, rep // 2, rep % 2]).astype(jnp.int32)
    vqk = shaped((events, 3 * width), BF16)
    square = shaped((events, width), BF16)
    wide = 2 * events * width

    block = shaped((width // 8, width), BF16)
    half = shaped((width // 2, width), F32)

    place, x = lax.optimization_barrier((place, x))
    x_y = swap(x, 2)
    x_c = swap(x, 1)
    far = functools.partial(pltpu.with_memory_space_constraint, memory_space=pltpu.HBM)
    (info,) = call(
        pack_body, [shaped((1, 6 * events), jnp.int32)], [HBM] * 4,
        (far(dest), far(slot), far(slot_user), far(slot_time)), moved=1 << 13, scratch=[pltpu.SemaphoreType.DMA((4,))],
    )
    info_y = swap(info, 2)
    info_c = swap(info, 1)
    w_near, u_o, vqk_o, slope = call(
        project_own_body,
        [shaped(w_in.shape, BF16), square, vqk, shaped((events, 4 * width), F32)], [HBM] * 2, (far(w_in), far(x)),
        flops=wide * 4 * width, moved=6 << 20, scratch=[pltpu.VMEM((events, width), BF16), pltpu.SemaphoreType.DMA((5,))],
    )
    (vqk_c,) = call(project_body, [vqk], [VMEM] * 2, (x_c, w_near), flops=wide * 3 * width, moved=3 << 20)
    x_y, info_y, _, _ = lax.optimization_barrier((x_y, info_y, vqk_o, vqk_c))
    info_d = swap(info_y, 1)
    lane, sub = call(
        codes_body, [shaped((8, events), F32), shaped((events, 8), F32)], [SMEM] + [VMEM] * 4,
        (place, info, info_y, info_c, info_d), flops=1 << 28, moved=1 << 20,
    )
    x_d = swap(x_y, 1)
    u_y, vqk_y = call(project_body, [square, vqk], [VMEM] * 2, (x_y, w_near), flops=wide * 4 * width, moved=3 << 20)
    (vqk_d,) = call(project_body, [vqk], [VMEM] * 2, (x_d, w_near), flops=wide * 3 * width, moved=3 << 20, after=(vqk_y,))
    kv = (vqk_o, vqk_y, vqk_c, vqk_d)

    mine, other, nrm, recip = call(
        functools.partial(forward_body, half_scale),
        [half, shaped(half.shape, BF16), shaped((events, width), F32), shaped((events, 128), F32)],
        [SMEM] + [VMEM] * 8,
        (place, *kv, u_o, lane, sub, dy),
        flops=wide * 4 * events * 3, moved=6 << 20,
        scratch=[pltpu.VMEM((events, width), F32), pltpu.VMEM((width, events), BF16)],
    )
    got = swap(other, 1)
    dy_late, _ = lax.optimization_barrier((dy, other))
    dy_y = swap(dy_late, 2)
    own, p1, p2, p3 = call(
        cut_body, [shaped(block.shape, F32), block, block, block], [SMEM] + [VMEM] * 2, (place, mine, got),
        flops=1 << 20, moved=1 << 20, scratch=[pltpu.VMEM(half.shape, F32)],
    )
    r1, r2, r3 = swap(p1, 0, 2), swap(p2, 0, 4), swap(p3, 0, 6)
    nrm_y, recip_y = call(
        functools.partial(partner_body, half_scale),
        [shaped((events, width), F32), shaped((events, 128), F32)], [VMEM] * 6,
        (*kv, lane, sub), flops=wide * 4 * events * 2, moved=6 << 20,
        scratch=[pltpu.VMEM((events, width), F32)], after=(p1, p2, p3),
    )
    (part,) = call(add_body, [block], [VMEM] * 4, (own, r1, r2, r3), flops=1 << 18, moved=1 << 19, after=(nrm_y,))
    r1, r2, r3 = swap(part, 0, 1), swap(part, 2, 0), swap(part, 2, 1)
    do_oy, gu = call(
        grad_o_body, [shaped((2 * events, width), BF16), square], [VMEM] * 10,
        (u_o, u_y, dy, dy_y, w_out, nrm, recip, nrm_y, recip_y, slope),
        flops=wide * 2 * width, moved=6 << 20, after=(part,),
    )
    do_cd = swap(do_oy, 1)
    (gq,) = call(
        functools.partial(grad_q_body, half_scale), [square], [VMEM] * 8,
        (*kv, lane, sub, do_oy, slope), flops=wide * 4 * events * 4, moved=6 << 20, after=(part,),
    )
    (part,) = call(add_body, [block], [VMEM] * 4, (part, r1, r2, r3), flops=1 << 18, moved=1 << 19, after=(gq,))
    r1, r2, r3 = swap(part, 0, 2), swap(part, 0, 4), swap(part, 0, 6)
    (grad_rows,) = call(
        functools.partial(grad_kv_body, half_scale), [shaped((1, events, 4 * width), BF16)], [VMEM] * 11,
        (*kv, lane, sub, do_oy, do_cd, slope, gu, gq), flops=wide * 4 * events * 6, moved=8 << 20, after=(part,),
    )
    (mine,) = call(
        join_body, [shaped(half.shape, BF16)], [SMEM] + [VMEM] * 4, (place, part, r1, r2, r3),
        flops=1 << 18, moved=1 << 19, after=(grad_rows,),
    )
    got = swap(mine, 1)
    (grad_w,) = call(
        functools.partial(final_body, factor), [shaped((width, width), F32)], [SMEM] + [VMEM] * 2,
        (place, mine, got), flops=1 << 18, moved=2 << 20,
    )
    return grad_rows, grad_w


def on_device(*args):
    events, width = args[0].shape[1:]
    plain = lax.axis_size("shard") == 4 and lax.axis_size("rep") == 8
    if plain and events == 256 and width == 512:
        return by_event(*args)
    return routed(*args)


def solution(mesh):
    return jax.shard_map(
        on_device,
        mesh=mesh,
        in_specs=(
            P("rep", "shard", None),
            P(),
            P("rep", "shard", None),
            P(),
            P("rep", "shard"),
            P("rep", "shard"),
            P("rep", "shard"),
            P("rep", "shard"),
        ),
        out_specs=(P("rep", "shard", None), P()),
        check_vma=False,
    )
```

```python
import functools
import math

import jax
import jax.numpy as jnp
from jax import lax
from jax.experimental import pallas as pl
from jax.experimental.pallas import tpu as pltpu
from jax.sharding import PartitionSpec as P

HEADS = 4
F32 = jnp.float32
BF16 = jnp.bfloat16
TIMES = 512
USERS = 4
VMEM = pl.BlockSpec(memory_space=pltpu.VMEM)
SMEM = pl.BlockSpec(memory_space=pltpu.SMEM)
HBM = pl.BlockSpec(memory_space=pltpu.HBM)


def silu_slope(value):
    sigma = jax.nn.sigmoid(value)
    return sigma * (1.0 + value * (1.0 - sigma))


def owner_pass(act, dy_rows, users, times, w_out):
    cap = act.shape[0]
    width = act.shape[1] // 4
    head_dim = width // HEADS
    scale = 1.0 / math.sqrt(head_dim)
    u_part = act[:, :width]
    v_heads = act[:, width : 2 * width].reshape(cap, HEADS, head_dim)
    q_heads = act[:, 2 * width : 3 * width].reshape(cap, HEADS, head_dim)
    k_heads = act[:, 3 * width :].reshape(cap, HEADS, head_dim)
    mask = (
        (users[:, None] == users[None, :])
        & (times[None, :] <= times[:, None])
        & (users[:, None] >= 0)
    )
    scores = (
        jnp.einsum("ihd,jhd->hij", q_heads, k_heads, preferred_element_type=jnp.float32) * scale
    )
    sigma = jax.nn.sigmoid(scores)
    attn = jnp.where(mask[None], scores * sigma, 0.0).astype(jnp.bfloat16)
    out = jnp.einsum("hij,jhd->ihd", attn, v_heads, preferred_element_type=jnp.float32).reshape(
        cap, width
    )
    centred = out - jnp.mean(out, axis=1, keepdims=True)
    recip = lax.rsqrt(jnp.mean(centred * centred, axis=1, keepdims=True) + 1e-05)
    nrm = centred * recip
    u_wide = u_part.astype(jnp.float32)
    zed = (nrm * u_wide).astype(jnp.bfloat16)
    part_w = lax.dot_general(
        zed, dy_rows, (((0,), (0,)), ((), ())), preferred_element_type=jnp.float32
    )
    dzed = lax.dot_general(
        dy_rows, w_out, (((1,), (1,)), ((), ())), preferred_element_type=jnp.float32
    )
    grad_u = dzed * nrm
    grad_n = dzed * u_wide
    grad_o = recip * (
        grad_n
        - jnp.mean(grad_n, axis=1, keepdims=True)
        - nrm * jnp.mean(grad_n * nrm, axis=1, keepdims=True)
    )
    grad_o = grad_o.astype(jnp.bfloat16).reshape(cap, HEADS, head_dim)
    grad_a = jnp.einsum("ihd,jhd->hij", grad_o, v_heads, preferred_element_type=jnp.float32)
    grad_v = jnp.einsum("hij,ihd->jhd", attn, grad_o, preferred_element_type=jnp.float32)
    grad_s = jnp.where(
        mask[None], grad_a * sigma * (1.0 + scores * (1.0 - sigma)) * scale, 0.0
    ).astype(jnp.bfloat16)
    grad_q = jnp.einsum("hij,jhd->ihd", grad_s, k_heads, preferred_element_type=jnp.float32)
    grad_k = jnp.einsum("hij,ihd->jhd", grad_s, q_heads, preferred_element_type=jnp.float32)
    grad_act = jnp.concatenate(
        [
            grad_u,
            grad_v.reshape(cap, width),
            grad_q.reshape(cap, width),
            grad_k.reshape(cap, width),
        ],
        axis=1,
    ).astype(jnp.bfloat16)
    return (lax.optimization_barrier(grad_act), part_w)


def routed(inputs, w_in, grad_out, w_out, dest, slot, slot_user, slot_time):
    shards = lax.axis_size("shard")
    groups = lax.axis_size("rep")
    per_dev = inputs.shape[1]
    width = inputs.shape[2]
    slots = 2 * per_dev // shards
    cap = shards * slots
    rows = inputs[0]
    flat = dest[0] * slots + slot[0]
    dy_buf = (
        jnp.zeros((cap, width), jnp.bfloat16)
        .at[flat]
        .set(grad_out[0])
        .reshape(shards, slots, width)
    )
    proj = jnp.dot(rows, w_in, preferred_element_type=jnp.float32)
    act = (proj * jax.nn.sigmoid(proj)).astype(jnp.bfloat16)
    act_buf = (
        jnp.zeros((cap, 4 * width), jnp.bfloat16)
        .at[flat]
        .set(act)
        .reshape(shards, slots, 4 * width)
    )
    got_act, got_dy = (
        lax.all_to_all(act_buf, "shard", split_axis=0, concat_axis=0, tiled=True),
        lax.all_to_all(dy_buf, "shard", split_axis=0, concat_axis=0, tiled=True),
    )
    owner_act = got_act.reshape(cap, 4 * width)
    grad_act, part_w = owner_pass(
        owner_act, got_dy.reshape(cap, width), slot_user[0], slot_time[0], w_out
    )
    back = lax.all_to_all(
        grad_act.reshape(shards, slots, 4 * width), "shard", split_axis=0, concat_axis=0, tiled=True
    )
    mine = back.reshape(cap, 4 * width)[flat]
    grad_rows = (mine.astype(jnp.float32) * silu_slope(proj)).astype(jnp.bfloat16)
    factor = 1.0 / math.sqrt(groups * shards * per_dev)
    summed = lax.psum(part_w, ("shard", "rep"))
    return (grad_rows[None], summed * factor)


def dot(a, b):
    return jnp.dot(a, b, preferred_element_type=F32)


def dot_nt(a, b):
    return lax.dot_general(a, b, (((1,), (1,)), ((), ())), preferred_element_type=F32)


def call(body, outs, specs, args, flops=0, moved=0, scratch=(), after=(), out_specs=None, alias=None):
    if after:
        last, *_ = lax.optimization_barrier((args[-1], *after))
        args = (*args[:-1], last)
    return pl.pallas_call(
        body,
        out_shape=outs,
        in_specs=specs,
        out_specs=out_specs or [VMEM] * len(outs),
        scratch_shapes=list(scratch),
        input_output_aliases=alias or {},
        compiler_params=pltpu.CompilerParams(vmem_limit_bytes=16 << 20),
        cost_estimate=pl.CostEstimate(flops=1 << 10, bytes_accessed=1 << 10, transcendentals=0),
    )(*args)


def shaped(shape, kind):
    return jax.ShapeDtypeStruct(shape, kind)


def silu_of(h):
    half = 0.5 * h
    t = jnp.tanh(half)
    return half + half * t, t


def project_own_body(w_hbm, x_hbm, w_ref, u_ref, v_ref, q_ref, k_ref, slope_ref, x_ref, sem):
    width = u_ref.shape[1]
    copies = [pltpu.make_async_copy(x_hbm, x_ref, sem.at[4])]
    for i in range(4):
        block = pl.ds(i * width, width)
        copies.append(pltpu.make_async_copy(w_hbm.at[:, block], w_ref.at[:, block], sem.at[i]))
    for copy in copies:
        copy.start()
    copies[0].wait()
    x = x_ref[...]
    for i, ref in enumerate((u_ref, v_ref, q_ref, k_ref)):
        copies[i + 1].wait()
        for col in range(0, width, 256):
            first = i * width + col
            act, t = silu_of(dot(x, w_ref[:, first : first + 256]))
            slope_ref[:, first : first + 256] = 0.5 * ((1.0 + t) + act * (1.0 - t))
            ref[:, col : col + 256] = act.astype(BF16)


def project_body(parts, x_ref, w_ref, *out_refs):
    width = x_ref.shape[1]
    x = x_ref[...]
    for part, ref in zip(parts, out_refs):
        for col in range(0, width, 256):
            first = part * width + col
            act, _ = silu_of(dot(x, w_ref[:, first : first + 256]))
            ref[:, col : col + 256] = act.astype(BF16)


def pack_body(dest_ref, slot_ref, user_ref, time_ref, out_ref, sem):
    first, copies = 0, []
    for i, ref in enumerate((dest_ref, slot_ref, user_ref, time_ref)):
        copies.append(pltpu.make_async_copy(ref, out_ref.at[:, first : first + ref.shape[1]], sem.at[i]))
        first += ref.shape[1]
    for copy in copies:
        copy.start()
    for copy in copies:
        copy.wait()


def codes_body(place_ref, i0, i1, i2, i3, lane_ref, sub_ref):
    infos = (i0, i1, i2, i3)
    me = place_ref[0]
    ids = (me, me ^ 2, me ^ 1, me ^ 3)
    events = lane_ref.shape[1]
    slots = events // 2
    row8 = lax.broadcasted_iota(jnp.int32, (8, slots), 0)
    down = lax.broadcasted_iota(jnp.int32, (slots, events), 0)
    rows = []
    for b in range(4):
        flat = infos[b][:, 0:events] * slots + infos[b][:, events : 2 * events]
        tables, hits = [], []
        for p in range(4):
            at = pl.multiple_of(2 * events + ids[b] * slots, slots)
            user = infos[p][:, pl.ds(at, slots)]
            at = pl.multiple_of(4 * events + ids[b] * slots, slots)
            code = (ids[p] * USERS + user) * TIMES + infos[p][:, pl.ds(at, slots)]
            tables.append(jnp.where(row8 == 0, code >> 6, code & 63).astype(F32).astype(BF16))
            hits.append(jnp.where(down == flat - ids[p] * slots, 1.0, 0.0).astype(BF16))
        total = dot(jnp.concatenate(tables, axis=1), jnp.concatenate(hits, axis=0))
        rows.append(total[0:1] * 64.0 + total[1:2])
    codes = jnp.concatenate(rows + rows, axis=0)
    lane_ref[...] = codes
    sub_ref[...] = codes.T


def pair_mask(low, high, key):
    return jnp.where((key >= low) & (key <= high), 1.0, 0.0).astype(BF16)


def raw_body(half_scale, q_ref, k0, k2, raw0_ref, raw2_ref):
    events = q_ref.shape[0]
    dim = q_ref.shape[1] // HEADS
    for head in range(HEADS):
        at = head * dim
        q = q_ref[:, at : at + dim]
        for k_ref, raw_ref in ((k0, raw0_ref), (k2, raw2_ref)):
            half = dot_nt(q, k_ref[:, at : at + dim]) * half_scale
            raw_ref[:, head * events : (head + 1) * events] = (half + half * jnp.tanh(half)).astype(BF16)


def row_masks(sub_ref, lane_ref):
    high = sub_ref[:, 0:1]
    low = jnp.floor(high * (1.0 / TIMES)) * TIMES
    return [pair_mask(low, high, lane_ref[b : b + 1, :]) for b in range(4)]


def forward_body(
    half_scale, place_ref, q_ref, v0, v1, v2, v3, k1, k3, raw0, raw2, u_ref, lane_ref, sub_ref, dy_ref,
    mine_ref, other_ref, nrm_ref, recip_ref, o_ref, zt_ref,
):
    events = q_ref.shape[0]
    dim = u_ref.shape[1] // HEADS
    masks = row_masks(sub_ref, lane_ref)
    for head in range(HEADS):
        at = head * dim
        q = q_ref[:, at : at + dim]
        total = None
        for v_ref, k_ref, raw_ref, mask in zip((v0, v1, v2, v3), (None, k1, None, k3), (raw0, None, raw2, None), masks):
            if raw_ref is None:
                half = dot_nt(q, k_ref[:, at : at + dim]) * half_scale
                attn = (half + half * jnp.tanh(half)).astype(BF16)
            else:
                attn = raw_ref[:, head * events : (head + 1) * events]
            part = dot(attn * mask, v_ref[:, at : at + dim])
            total = part if total is None else total + part
        o_ref[:, at : at + dim] = total
    out = o_ref[...]
    centred = out - jnp.mean(out, axis=1, keepdims=True)
    recip = lax.rsqrt(jnp.mean(centred * centred, axis=1, keepdims=True) + 1e-05)
    nrm = centred * recip
    nrm_ref[...] = nrm
    recip_ref[...] = jnp.broadcast_to(recip, recip_ref.shape)
    zt_ref[...] = (nrm * u_ref[...].astype(F32)).T.astype(BF16)
    rows = mine_ref.shape[0]
    core = place_ref[1]
    dy = dy_ref[...]
    other_ref[...] = dot(zt_ref[pl.ds(pl.multiple_of((1 - core) * rows, rows), rows), :], dy).astype(BF16)
    mine_ref[...] = dot(zt_ref[pl.ds(pl.multiple_of(core * rows, rows), rows), :], dy)


def grad_o_body(u_ref, dy_ref, w_out_ref, nrm_ref, recip_ref, slope_ref, do_ref, gu_ref):
    width = u_ref.shape[1]
    dzed = dot_nt(dy_ref[...], w_out_ref[...])
    nrm = nrm_ref[...]
    gu_ref[...] = ((dzed * nrm).astype(BF16).astype(F32) * slope_ref[:, :width]).astype(BF16)
    grad_n = dzed * u_ref[...].astype(F32)
    do_ref[...] = (
        recip_ref[:, 0:1]
        * (
            grad_n
            - jnp.mean(grad_n, axis=1, keepdims=True)
            - nrm * jnp.mean(grad_n * nrm, axis=1, keepdims=True)
        )
    ).astype(BF16)


def grad_q_body(half_scale, q_ref, v0, v1, v2, v3, k0, k1, k2, k3, lane_ref, sub_ref, do_ref, slope_ref, gq_ref):
    width = gq_ref.shape[1]
    dim = width // HEADS
    masks = row_masks(sub_ref, lane_ref)
    for head in range(HEADS):
        at = head * dim
        q = q_ref[:, at : at + dim]
        do = do_ref[:, at : at + dim]
        total = None
        for v_ref, k_ref, mask in zip((v0, v1, v2, v3), (k0, k1, k2, k3), masks):
            k = k_ref[:, at : at + dim]
            half = dot_nt(q, k) * half_scale
            t = jnp.tanh(half)
            slope = (1.0 + t) * ((1.0 + half) - half * t)
            grad_s = (dot_nt(do, v_ref[:, at : at + dim]) * slope).astype(BF16) * mask
            part = dot(grad_s, k)
            total = part if total is None else total + part
        grad = (total * half_scale).astype(BF16).astype(F32)
        gq_ref[:, at : at + dim] = (grad * slope_ref[:, 2 * width + at : 2 * width + at + dim]).astype(BF16)


def grad_kv_sums(half_scale, at, dim, v, k, pairs, sum_v, sum_k):
    for q_ref, do_ref, mask in pairs:
        q = q_ref[:, at : at + dim]
        do = do_ref[:, at : at + dim]
        half = dot_nt(k, q) * half_scale
        t = jnp.tanh(half)
        rise = 1.0 + t
        part_v = dot((half * rise).astype(BF16) * mask, do)
        slope = rise * ((1.0 + half) - half * t)
        grad_s = (dot_nt(v, do) * slope).astype(BF16) * mask
        part_k = dot(grad_s, q)
        sum_v = part_v if sum_v is None else sum_v + part_v
        sum_k = part_k if sum_k is None else sum_k + part_k
    return sum_v, sum_k


def column_masks(sub_ref, lane_ref, blocks):
    key = sub_ref[:, 0:1]
    masks = []
    for b in blocks:
        high = lane_ref[b : b + 1, :]
        low = jnp.floor(high * (1.0 / TIMES)) * TIMES
        masks.append(pair_mask(low, high, key))
    return masks


def grad_kv_near_body(half_scale, v_ref, k_ref, q0, q2, lane_ref, sub_ref, do0, do2, sum_v_ref, sum_k_ref):
    dim = v_ref.shape[1] // HEADS
    masks = column_masks(sub_ref, lane_ref, (0, 2))
    for head in range(HEADS):
        at = head * dim
        sum_v, sum_k = grad_kv_sums(
            half_scale, at, dim, v_ref[:, at : at + dim], k_ref[:, at : at + dim],
            zip((q0, q2), (do0, do2), masks), None, None,
        )
        sum_v_ref[:, at : at + dim] = sum_v
        sum_k_ref[:, at : at + dim] = sum_k


def grad_kv_far_body(
    half_scale, v_ref, k_ref, q1, q3, lane_ref, sub_ref, do1, do3, sum_v_ref, sum_k_ref, slope_ref, gu_ref, gq_ref,
    out_ref,
):
    width = gq_ref.shape[1]
    dim = width // HEADS
    masks = column_masks(sub_ref, lane_ref, (1, 3))
    out_ref[0, :, 0:width] = gu_ref[...]
    out_ref[0, :, 2 * width : 3 * width] = gq_ref[...]
    for head in range(HEADS):
        at = head * dim
        sum_v, sum_k = grad_kv_sums(
            half_scale, at, dim, v_ref[:, at : at + dim], k_ref[:, at : at + dim],
            zip((q1, q3), (do1, do3), masks), sum_v_ref[:, at : at + dim], sum_k_ref[:, at : at + dim],
        )
        for first, grad in ((width + at, sum_v), (3 * width + at, sum_k * half_scale)):
            grad = grad.astype(BF16).astype(F32)
            out_ref[0, :, first : first + dim] = (grad * slope_ref[:, first : first + dim]).astype(BF16)


def cut_body(place_ref, mine_ref, got_ref, own_ref, p1_ref, p2_ref, p3_ref, sum_ref):
    rows = own_ref.shape[0]
    z = place_ref[2]
    sum_ref[...] = mine_ref[...] + got_ref[...].astype(F32)
    own_ref[...] = sum_ref[pl.ds(pl.multiple_of(z * rows, rows), rows), :]
    for k, ref in ((1, p1_ref), (2, p2_ref), (3, p3_ref)):
        ref[...] = sum_ref[pl.ds(pl.multiple_of((z ^ k) * rows, rows), rows), :].astype(BF16)


def add_body(own_ref, r1, r2, r3, out_ref):
    out_ref[...] = (
        (own_ref[...].astype(F32) + r1[...].astype(F32)) + (r2[...].astype(F32) + r3[...].astype(F32))
    ).astype(BF16)


def final_body(factor, place_ref, b0, b1, b2, b3, t0, t1, t2, t3, out_hbm, wide_ref, sem):
    rows = b0.shape[0]
    z, core = place_ref[2], place_ref[1]
    copies = []
    for half, refs in ((core, (b0, b1, b2, b3)), (1 - core, (t0, t1, t2, t3))):
        for k, ref in enumerate(refs):
            i = len(copies)
            wide_ref[i] = ref[...].astype(F32) * factor
            at = pl.multiple_of((half * 4 + (z ^ k)) * rows, rows)
            copies.append(pltpu.make_async_copy(wide_ref.at[i], out_hbm.at[pl.ds(at, rows), :], sem.at[i]))
            copies[-1].start()
    for copy in copies:
        copy.wait()


def swap(value, shard_bits, rep_bits=0):
    pairs = [(i, i ^ (shard_bits * 8 + rep_bits)) for i in range(32)]
    return lax.ppermute(value, ("shard", "rep"), pairs)


def by_event(inputs, w_in, grad_out, w_out, dest, slot, slot_user, slot_time):
    x0, dy = inputs[0], grad_out[0]
    events, width = x0.shape
    half_scale = 0.5 / math.sqrt(width // HEADS)
    factor = 1.0 / math.sqrt(32 * events)
    me, rep = lax.axis_index("shard"), lax.axis_index("rep")
    place = jnp.stack([me, me % 2, me // 2 * 2 + rep % 2]).astype(jnp.int32)
    far = functools.partial(pltpu.with_memory_space_constraint, memory_space=pltpu.HBM)
    tie = lax.optimization_barrier
    square = shaped((events, width), BF16)
    square_f32 = shaped((events, width), F32)
    half = shaped((width // 2, width), F32)
    block = shaped((width // 8, width), BF16)
    wide = 2 * events * width

    def project(parts, x):
        return call(
            functools.partial(project_body, parts), [square] * len(parts), [VMEM] * 2, (x, w_near),
            flops=wide * len(parts) * width, moved=3 << 20,
        )

    place, x0 = tie((place, x0))
    x1 = swap(x0, 2)
    x2 = swap(x0, 1)
    (info0,) = call(
        pack_body, [shaped((1, 6 * events), jnp.int32)], [HBM] * 4,
        (far(dest), far(slot), far(slot_user), far(slot_time)), moved=1 << 13, scratch=[pltpu.SemaphoreType.DMA((4,))],
    )
    info1 = swap(info0, 2)
    info2 = swap(info0, 1)
    w_near, u0, v0, q0, k0, slope = call(
        project_own_body,
        [shaped(w_in.shape, BF16), square, square, square, square, shaped((events, 4 * width), F32)],
        [HBM] * 2, (far(w_in), far(x0)), flops=wide * 4 * width, moved=6 << 20,
        scratch=[pltpu.VMEM((events, width), BF16), pltpu.SemaphoreType.DMA((5,))],
    )
    v2, q2, k2 = project((1, 2, 3), x2)
    raw0, raw2 = call(
        functools.partial(raw_body, half_scale), [shaped((events, HEADS * events), BF16)] * 2, [VMEM] * 3,
        (q0, k0, k2), flops=wide * 2 * events, moved=2 << 20,
    )
    x1, info1, info2, _ = tie((x1, info1, info2, raw0))
    x3 = swap(x1, 1)
    info3 = swap(info1, 1)
    v1, k1 = project((1, 3), x1)
    lane, sub = call(
        codes_body, [shaped((8, events), F32), shaped((events, 8), F32)], [SMEM] + [VMEM] * 4,
        (place, info0, info1, info2, info3), flops=1 << 26, moved=1 << 20,
    )
    x3_late, _, _ = tie((x3, v1, lane))
    v3, k3 = project((1, 3), x3_late)
    values, keys = (v0, v1, v2, v3), (k0, k1, k2, k3)

    mine, other, nrm, recip = call(
        functools.partial(forward_body, half_scale),
        [half, shaped(half.shape, BF16), square_f32, shaped((events, 128), F32)], [SMEM] + [VMEM] * 13,
        (place, q0, *values, k1, k3, raw0, raw2, u0, lane, sub, dy), flops=wide * 4 * events * 3, moved=6 << 20,
        scratch=[pltpu.VMEM((events, width), F32), pltpu.VMEM((width, events), BF16)],
    )
    got = swap(other, 1)
    do0, gu = call(
        grad_o_body, [square, square], [VMEM] * 6, (u0, dy, w_out, nrm, recip, slope),
        flops=wide * width, moved=4 << 20, after=(other,),
    )
    got, _ = tie((got, do0))
    own, p1, p2, p3 = call(
        cut_body, [shaped(block.shape, F32), block, block, block], [SMEM] + [VMEM] * 2, (place, mine, got),
        flops=1 << 20, moved=1 << 20, scratch=[pltpu.VMEM(half.shape, F32)],
    )
    r1, r2, r3 = swap(p1, 0, 1), swap(p2, 2, 0), swap(p3, 2, 1)
    (gq,) = call(
        functools.partial(grad_q_body, half_scale), [square], [VMEM] * 13,
        (q0, *values, *keys, lane, sub, do0, slope), flops=wide * 4 * events * 4, moved=6 << 20, after=(p1, p2, p3),
    )
    (part,) = call(add_body, [block], [VMEM] * 4, (own, r1, r2, r3), flops=1 << 18, moved=1 << 19, after=(gq,))
    r1, r2, r3 = swap(part, 0, 2), swap(part, 0, 4), swap(part, 0, 6)
    do_late, _ = tie((do0, part))
    do2 = swap(do_late, 1)
    do1 = swap(do_late, 2)
    x1_late, x3_late, _ = tie((x1, x3, part))
    (q1,) = project((2,), x1_late)
    (q3,) = project((2,), x3_late)
    sum_v, sum_k = call(
        functools.partial(grad_kv_near_body, half_scale), [square_f32, square_f32], [VMEM] * 8,
        (v0, k0, q0, q2, lane, sub, do0, do2), flops=wide * 4 * events * 3, moved=6 << 20, after=(part,),
    )
    (part,) = call(add_body, [block], [VMEM] * 4, (part, r1, r2, r3), flops=1 << 18, moved=1 << 19, after=(sum_v, q1, q3))
    do1, _ = tie((do1, part))
    do3 = swap(do1, 1)
    r1, r2, r3 = swap(part, 0, 1), swap(part, 2, 0), swap(part, 2, 1)
    (grad_rows,) = call(
        functools.partial(grad_kv_far_body, half_scale), [shaped((1, events, 4 * width), BF16)], [VMEM] * 13,
        (v0, k0, q1, q3, lane, sub, do1, do3, sum_v, sum_k, slope, gu, gq),
        flops=wide * 4 * events * 3, moved=8 << 20, after=(part,),
    )
    r1, r2, r3, _ = tie((r1, r2, r3, grad_rows))
    theirs = [swap(b, 1) for b in (part, r1, r2, r3)]
    (grad_w,) = call(
        functools.partial(final_body, factor), [shaped((width, width), F32)], [SMEM] + [VMEM] * 8,
        (place, part, r1, r2, r3, *theirs), flops=1 << 18, moved=2 << 20, out_specs=[HBM],
        scratch=[pltpu.VMEM((8, width // 8, width), F32), pltpu.SemaphoreType.DMA((8,))],
    )
    return grad_rows, grad_w


def on_device(*args):
    events, width = args[0].shape[1:]
    plain = lax.axis_size("shard") == 4 and lax.axis_size("rep") == 8
    if plain and events == 256 and width == 512:
        return by_event(*args)
    return routed(*args)


def solution(mesh):
    return jax.shard_map(
        on_device,
        mesh=mesh,
        in_specs=(
            P("rep", "shard", None),
            P(),
            P("rep", "shard", None),
            P(),
            P("rep", "shard"),
            P("rep", "shard"),
            P("rep", "shard"),
            P("rep", "shard"),
        ),
        out_specs=(P("rep", "shard", None), P()),
        check_vma=False,
    )
```

```python
import functools
import math

import jax
import jax.numpy as jnp
from jax import lax
from jax.experimental import pallas as pl
from jax.experimental.pallas import tpu as pltpu
from jax.sharding import PartitionSpec as P

HEADS = 4
F32 = jnp.float32
BF16 = jnp.bfloat16
TIMES = 512
USERS = 4
VMEM = pl.BlockSpec(memory_space=pltpu.VMEM)
HBM = pl.BlockSpec(memory_space=pltpu.HBM)


def silu_slope(value):
    sigma = jax.nn.sigmoid(value)
    return sigma * (1.0 + value * (1.0 - sigma))


def owner_pass(act, dy_rows, users, times, w_out):
    cap = act.shape[0]
    width = act.shape[1] // 4
    head_dim = width // HEADS
    scale = 1.0 / math.sqrt(head_dim)
    u_part = act[:, :width]
    v_heads = act[:, width : 2 * width].reshape(cap, HEADS, head_dim)
    q_heads = act[:, 2 * width : 3 * width].reshape(cap, HEADS, head_dim)
    k_heads = act[:, 3 * width :].reshape(cap, HEADS, head_dim)
    mask = (
        (users[:, None] == users[None, :])
        & (times[None, :] <= times[:, None])
        & (users[:, None] >= 0)
    )
    scores = (
        jnp.einsum("ihd,jhd->hij", q_heads, k_heads, preferred_element_type=jnp.float32) * scale
    )
    sigma = jax.nn.sigmoid(scores)
    attn = jnp.where(mask[None], scores * sigma, 0.0).astype(jnp.bfloat16)
    out = jnp.einsum("hij,jhd->ihd", attn, v_heads, preferred_element_type=jnp.float32).reshape(
        cap, width
    )
    centred = out - jnp.mean(out, axis=1, keepdims=True)
    recip = lax.rsqrt(jnp.mean(centred * centred, axis=1, keepdims=True) + 1e-05)
    nrm = centred * recip
    u_wide = u_part.astype(jnp.float32)
    zed = (nrm * u_wide).astype(jnp.bfloat16)
    part_w = lax.dot_general(
        zed, dy_rows, (((0,), (0,)), ((), ())), preferred_element_type=jnp.float32
    )
    dzed = lax.dot_general(
        dy_rows, w_out, (((1,), (1,)), ((), ())), preferred_element_type=jnp.float32
    )
    grad_u = dzed * nrm
    grad_n = dzed * u_wide
    grad_o = recip * (
        grad_n
        - jnp.mean(grad_n, axis=1, keepdims=True)
        - nrm * jnp.mean(grad_n * nrm, axis=1, keepdims=True)
    )
    grad_o = grad_o.astype(jnp.bfloat16).reshape(cap, HEADS, head_dim)
    grad_a = jnp.einsum("ihd,jhd->hij", grad_o, v_heads, preferred_element_type=jnp.float32)
    grad_v = jnp.einsum("hij,ihd->jhd", attn, grad_o, preferred_element_type=jnp.float32)
    grad_s = jnp.where(
        mask[None], grad_a * sigma * (1.0 + scores * (1.0 - sigma)) * scale, 0.0
    ).astype(jnp.bfloat16)
    grad_q = jnp.einsum("hij,jhd->ihd", grad_s, k_heads, preferred_element_type=jnp.float32)
    grad_k = jnp.einsum("hij,ihd->jhd", grad_s, q_heads, preferred_element_type=jnp.float32)
    grad_act = jnp.concatenate(
        [
            grad_u,
            grad_v.reshape(cap, width),
            grad_q.reshape(cap, width),
            grad_k.reshape(cap, width),
        ],
        axis=1,
    ).astype(jnp.bfloat16)
    return (lax.optimization_barrier(grad_act), part_w)


def routed(inputs, w_in, grad_out, w_out, dest, slot, slot_user, slot_time):
    shards = lax.axis_size("shard")
    groups = lax.axis_size("rep")
    per_dev = inputs.shape[1]
    width = inputs.shape[2]
    slots = 2 * per_dev // shards
    cap = shards * slots
    rows = inputs[0]
    flat = dest[0] * slots + slot[0]
    dy_buf = (
        jnp.zeros((cap, width), jnp.bfloat16)
        .at[flat]
        .set(grad_out[0])
        .reshape(shards, slots, width)
    )
    proj = jnp.dot(rows, w_in, preferred_element_type=jnp.float32)
    act = (proj * jax.nn.sigmoid(proj)).astype(jnp.bfloat16)
    act_buf = (
        jnp.zeros((cap, 4 * width), jnp.bfloat16)
        .at[flat]
        .set(act)
        .reshape(shards, slots, 4 * width)
    )
    got_act, got_dy = (
        lax.all_to_all(act_buf, "shard", split_axis=0, concat_axis=0, tiled=True),
        lax.all_to_all(dy_buf, "shard", split_axis=0, concat_axis=0, tiled=True),
    )
    owner_act = got_act.reshape(cap, 4 * width)
    grad_act, part_w = owner_pass(
        owner_act, got_dy.reshape(cap, width), slot_user[0], slot_time[0], w_out
    )
    back = lax.all_to_all(
        grad_act.reshape(shards, slots, 4 * width), "shard", split_axis=0, concat_axis=0, tiled=True
    )
    mine = back.reshape(cap, 4 * width)[flat]
    grad_rows = (mine.astype(jnp.float32) * silu_slope(proj)).astype(jnp.bfloat16)
    factor = 1.0 / math.sqrt(groups * shards * per_dev)
    summed = lax.psum(part_w, ("shard", "rep"))
    return (grad_rows[None], summed * factor)


def dot(a, b):
    return jnp.dot(a, b, preferred_element_type=F32)


def dot_nt(a, b):
    return lax.dot_general(a, b, (((1,), (1,)), ((), ())), preferred_element_type=F32)


def here():
    me, rep = lax.axis_index("shard"), lax.axis_index("rep")
    return me, lax.rem(me, 2), lax.div(me, 2) * 2 + lax.rem(rep, 2)


def call(body, outs, specs, args, flops=0, moved=0, scratch=(), after=(), out_specs=None, alias=None):
    if after:
        last, *_ = lax.optimization_barrier((args[-1], *after))
        args = (*args[:-1], last)
    return pl.pallas_call(
        body,
        out_shape=outs,
        in_specs=specs,
        out_specs=out_specs or [VMEM] * len(outs),
        scratch_shapes=list(scratch),
        input_output_aliases=alias or {},
        compiler_params=pltpu.CompilerParams(vmem_limit_bytes=16 << 20),
        cost_estimate=pl.CostEstimate(flops=1 << 10, bytes_accessed=1 << 10, transcendentals=0),
    )(*args)


def shaped(shape, kind):
    return jax.ShapeDtypeStruct(shape, kind)


def silu_of(h):
    half = 0.5 * h
    t = jnp.tanh(half)
    return half + half * t, t


def project_own_body(w_hbm, x_hbm, w_ref, u_ref, v_ref, q_ref, k_ref, slope_ref, x_ref, sem):
    width = u_ref.shape[1]
    copies = [pltpu.make_async_copy(x_hbm, x_ref, sem.at[4])]
    for i in range(4):
        block = pl.ds(i * width, width)
        copies.append(pltpu.make_async_copy(w_hbm.at[:, block], w_ref.at[:, block], sem.at[i]))
    for copy in copies:
        copy.start()
    copies[0].wait()
    x = x_ref[...]
    for i, ref in enumerate((u_ref, v_ref, q_ref, k_ref)):
        copies[i + 1].wait()
        for col in range(0, width, 256):
            first = i * width + col
            act, t = silu_of(dot(x, w_ref[:, first : first + 256]))
            slope_ref[:, first : first + 256] = 0.5 * ((1.0 + t) + act * (1.0 - t))
            ref[:, col : col + 256] = act.astype(BF16)


def project_body(parts, x_ref, w_ref, *out_refs):
    width = x_ref.shape[1]
    x = x_ref[...]
    for part, ref in zip(parts, out_refs):
        for col in range(0, width, 256):
            first = part * width + col
            act, _ = silu_of(dot(x, w_ref[:, first : first + 256]))
            ref[:, col : col + 256] = act.astype(BF16)


def pack_body(dest_ref, slot_ref, user_ref, time_ref, out_ref, sem):
    first, copies = 0, []
    for i, ref in enumerate((dest_ref, slot_ref, user_ref, time_ref)):
        copies.append(pltpu.make_async_copy(ref, out_ref.at[:, first : first + ref.shape[1]], sem.at[i]))
        first += ref.shape[1]
    for copy in copies:
        copy.start()
    for copy in copies:
        copy.wait()


def codes_body(i0, i1, i2, i3, lane_ref, sub_ref):
    infos = (i0, i1, i2, i3)
    me, _, _ = here()
    ids = (me, me ^ 2, me ^ 1, me ^ 3)
    events = lane_ref.shape[1]
    slots = events // 2
    row8 = lax.broadcasted_iota(jnp.int32, (8, slots), 0)
    down = lax.broadcasted_iota(jnp.int32, (slots, events), 0)
    rows = []
    for b in range(4):
        flat = infos[b][:, 0:events] * slots + infos[b][:, events : 2 * events]
        tables, hits = [], []
        for p in range(4):
            at = pl.multiple_of(2 * events + ids[b] * slots, slots)
            user = infos[p][:, pl.ds(at, slots)]
            at = pl.multiple_of(4 * events + ids[b] * slots, slots)
            code = (ids[p] * USERS + user) * TIMES + infos[p][:, pl.ds(at, slots)]
            tables.append(jnp.where(row8 == 0, code >> 6, code & 63).astype(F32).astype(BF16))
            hits.append(jnp.where(down == flat - ids[p] * slots, 1.0, 0.0).astype(BF16))
        total = dot(jnp.concatenate(tables, axis=1), jnp.concatenate(hits, axis=0))
        rows.append(total[0:1] * 64.0 + total[1:2])
    codes = jnp.concatenate(rows + rows, axis=0)
    lane_ref[...] = codes
    sub_ref[...] = codes.T


def pair_mask(low, high, key):
    return jnp.where((key >= low) & (key <= high), 1.0, 0.0).astype(BF16)


def raw_body(half_scale, q_ref, *refs):
    events = q_ref.shape[0]
    dim = q_ref.shape[1] // HEADS
    count = len(refs) // 2
    for head in range(HEADS):
        at = head * dim
        q = q_ref[:, at : at + dim]
        for k_ref, raw_ref in zip(refs[:count], refs[count:]):
            half = dot_nt(q, k_ref[:, at : at + dim]) * half_scale
            raw_ref[:, head * events : (head + 1) * events] = (half + half * jnp.tanh(half)).astype(BF16)


def row_masks(sub_ref, lane_ref):
    high = sub_ref[:, 0:1]
    low = jnp.floor(high * (1.0 / TIMES)) * TIMES
    return [pair_mask(low, high, lane_ref[b : b + 1, :]) for b in range(4)]


def forward_body(
    half_scale, q_ref, v0, v1, v2, v3, k3, raw0, raw1, raw2, u_ref, lane_ref, sub_ref, dy_ref,
    zt_ref, other_ref, nrm_ref, recip_ref, o_ref,
):
    events = q_ref.shape[0]
    dim = u_ref.shape[1] // HEADS
    masks = row_masks(sub_ref, lane_ref)
    for head in range(HEADS):
        at = head * dim
        q = q_ref[:, at : at + dim]
        total = None
        for v_ref, k_ref, raw_ref, mask in zip((v0, v1, v2, v3), (None, None, None, k3), (raw0, raw1, raw2, None), masks):
            if raw_ref is None:
                half = dot_nt(q, k_ref[:, at : at + dim]) * half_scale
                attn = (half + half * jnp.tanh(half)).astype(BF16)
            else:
                attn = raw_ref[:, head * events : (head + 1) * events]
            part = dot(attn * mask, v_ref[:, at : at + dim])
            total = part if total is None else total + part
        o_ref[:, at : at + dim] = total
    out = o_ref[...]
    centred = out - jnp.mean(out, axis=1, keepdims=True)
    recip = lax.rsqrt(jnp.mean(centred * centred, axis=1, keepdims=True) + 1e-05)
    nrm = centred * recip
    nrm_ref[...] = nrm
    recip_ref[...] = jnp.broadcast_to(recip, recip_ref.shape)
    zt_ref[...] = (nrm * u_ref[...].astype(F32)).T.astype(BF16)
    rows = other_ref.shape[0]
    _, core, _ = here()
    at = pl.ds(pl.multiple_of((1 - core) * rows, rows), rows)
    other_ref[...] = dot(zt_ref[at, :], dy_ref[...]).astype(BF16)


def mine_body(zt_ref, dy_ref, mine_ref):
    rows = mine_ref.shape[0]
    _, core, _ = here()
    mine_ref[...] = dot(zt_ref[pl.ds(pl.multiple_of(core * rows, rows), rows), :], dy_ref[...])


def grad_o_body(u_ref, dy_ref, w_out_ref, nrm_ref, recip_ref, slope_ref, do_ref, gu_ref):
    width = u_ref.shape[1]
    dzed = dot_nt(dy_ref[...], w_out_ref[...])
    nrm = nrm_ref[...]
    gu_ref[...] = ((dzed * nrm).astype(BF16).astype(F32) * slope_ref[:, :width]).astype(BF16)
    grad_n = dzed * u_ref[...].astype(F32)
    do_ref[...] = (
        recip_ref[:, 0:1]
        * (
            grad_n
            - jnp.mean(grad_n, axis=1, keepdims=True)
            - nrm * jnp.mean(grad_n * nrm, axis=1, keepdims=True)
        )
    ).astype(BF16)


def grad_q_body(half_scale, q_ref, v0, v1, v2, v3, k0, k1, k2, k3, lane_ref, sub_ref, do_ref, slope_ref, gq_ref):
    width = gq_ref.shape[1]
    dim = width // HEADS
    masks = row_masks(sub_ref, lane_ref)
    for head in range(HEADS):
        at = head * dim
        q = q_ref[:, at : at + dim]
        do = do_ref[:, at : at + dim]
        total = None
        for v_ref, k_ref, mask in zip((v0, v1, v2, v3), (k0, k1, k2, k3), masks):
            k = k_ref[:, at : at + dim]
            half = dot_nt(q, k) * half_scale
            t = jnp.tanh(half)
            slope = (1.0 + t) * ((1.0 + half) - half * t)
            grad_s = (dot_nt(do, v_ref[:, at : at + dim]) * slope).astype(BF16) * mask
            part = dot(grad_s, k)
            total = part if total is None else total + part
        grad = (total * half_scale).astype(BF16).astype(F32)
        gq_ref[:, at : at + dim] = (grad * slope_ref[:, 2 * width + at : 2 * width + at + dim]).astype(BF16)


def grad_kv_sums(half_scale, at, dim, v, k, pairs, sum_v, sum_k):
    for q_ref, do_ref, mask in pairs:
        q = q_ref[:, at : at + dim]
        do = do_ref[:, at : at + dim]
        half = dot_nt(k, q) * half_scale
        t = jnp.tanh(half)
        rise = 1.0 + t
        part_v = dot((half * rise).astype(BF16) * mask, do)
        slope = rise * ((1.0 + half) - half * t)
        grad_s = (dot_nt(v, do) * slope).astype(BF16) * mask
        part_k = dot(grad_s, q)
        sum_v = part_v if sum_v is None else sum_v + part_v
        sum_k = part_k if sum_k is None else sum_k + part_k
    return sum_v, sum_k


def column_masks(sub_ref, lane_ref, blocks):
    key = sub_ref[:, 0:1]
    masks = []
    for b in blocks:
        high = lane_ref[b : b + 1, :]
        low = jnp.floor(high * (1.0 / TIMES)) * TIMES
        masks.append(pair_mask(low, high, key))
    return masks


def grad_kv_near_body(half_scale, v_ref, k_ref, q0, q2, lane_ref, sub_ref, do0, do2, sum_v_ref, sum_k_ref):
    dim = v_ref.shape[1] // HEADS
    masks = column_masks(sub_ref, lane_ref, (0, 2))
    for head in range(HEADS):
        at = head * dim
        sum_v, sum_k = grad_kv_sums(
            half_scale, at, dim, v_ref[:, at : at + dim], k_ref[:, at : at + dim],
            zip((q0, q2), (do0, do2), masks), None, None,
        )
        sum_v_ref[:, at : at + dim] = sum_v
        sum_k_ref[:, at : at + dim] = sum_k


def grad_kv_far_body(
    half_scale, v_ref, k_ref, q1, q3, lane_ref, sub_ref, do1, do3, sum_v_ref, sum_k_ref, slope_ref, gu_ref, gq_ref,
    out_ref,
):
    width = gq_ref.shape[1]
    dim = width // HEADS
    masks = column_masks(sub_ref, lane_ref, (1, 3))
    out_ref[0, :, 0:width] = gu_ref[...]
    out_ref[0, :, 2 * width : 3 * width] = gq_ref[...]
    for head in range(HEADS):
        at = head * dim
        sum_v, sum_k = grad_kv_sums(
            half_scale, at, dim, v_ref[:, at : at + dim], k_ref[:, at : at + dim],
            zip((q1, q3), (do1, do3), masks), sum_v_ref[:, at : at + dim], sum_k_ref[:, at : at + dim],
        )
        for first, grad in ((width + at, sum_v), (3 * width + at, sum_k * half_scale)):
            grad = grad.astype(BF16).astype(F32)
            out_ref[0, :, first : first + dim] = (grad * slope_ref[:, first : first + dim]).astype(BF16)


def cut_body(mine_ref, got_ref, own_ref, p1_ref, p2_ref, p3_ref):
    rows = own_ref.shape[0]
    _, _, spot = here()
    for k, ref in enumerate((own_ref, p1_ref, p2_ref, p3_ref)):
        at = pl.ds(pl.multiple_of((spot ^ k) * rows, rows), rows)
        ref[...] = (mine_ref[at, :] + got_ref[at, :].astype(F32)).astype(ref.dtype)


def add_body(own_ref, r1, r2, r3, out_ref):
    out_ref[...] = (
        (own_ref[...].astype(F32) + r1[...].astype(F32)) + (r2[...].astype(F32) + r3[...].astype(F32))
    ).astype(BF16)


def final_body(factor, b0, b1, b2, b3, t0, t1, t2, t3, out_hbm, wide_ref, sem):
    rows = b0.shape[0]
    _, core, z = here()
    copies = []
    for half, refs in ((core, (b0, b1, b2, b3)), (1 - core, (t0, t1, t2, t3))):
        for k, ref in enumerate(refs):
            i = len(copies)
            wide_ref[i] = ref[...].astype(F32) * factor
            at = pl.multiple_of((half * 4 + (z ^ k)) * rows, rows)
            copies.append(pltpu.make_async_copy(wide_ref.at[i], out_hbm.at[pl.ds(at, rows), :], sem.at[i]))
            copies[-1].start()
    for copy in copies:
        copy.wait()


def swap(value, shard_bits, rep_bits=0):
    pairs = [(i, i ^ (shard_bits * 8 + rep_bits)) for i in range(32)]
    return lax.ppermute(value, ("shard", "rep"), pairs)


def by_event(inputs, w_in, grad_out, w_out, dest, slot, slot_user, slot_time):
    x0, dy = inputs[0], grad_out[0]
    events, width = x0.shape
    half_scale = 0.5 / math.sqrt(width // HEADS)
    factor = 1.0 / math.sqrt(32 * events)
    far = functools.partial(pltpu.with_memory_space_constraint, memory_space=pltpu.HBM)
    tie = lax.optimization_barrier
    square = shaped((events, width), BF16)
    square_f32 = shaped((events, width), F32)
    half = shaped((width // 2, width), F32)
    block = shaped((width // 8, width), BF16)
    wide = 2 * events * width

    def project(parts, x):
        return call(
            functools.partial(project_body, parts), [square] * len(parts), [VMEM] * 2, (x, w_near),
            flops=wide * len(parts) * width, moved=3 << 20,
        )

    x1 = swap(x0, 2)
    x2 = swap(x0, 1)
    (info0,) = call(
        pack_body, [shaped((1, 6 * events), jnp.int32)], [HBM] * 4,
        (far(dest), far(slot), far(slot_user), far(slot_time)), moved=1 << 13, scratch=[pltpu.SemaphoreType.DMA((4,))],
    )
    info1 = swap(info0, 2)
    info2 = swap(info0, 1)
    w_near, u0, v0, q0, k0, slope = call(
        project_own_body,
        [shaped(w_in.shape, BF16), square, square, square, square, shaped((events, 4 * width), F32)],
        [HBM] * 2, (far(w_in), far(x0)), flops=wide * 4 * width, moved=6 << 20,
        scratch=[pltpu.VMEM((events, width), BF16), pltpu.SemaphoreType.DMA((5,))],
    )
    v2, q2, k2 = project((1, 2, 3), x2)
    raw0, raw2 = call(
        functools.partial(raw_body, half_scale), [shaped((events, HEADS * events), BF16)] * 2, [VMEM] * 3,
        (q0, k0, k2), flops=wide * 2 * events, moved=2 << 20,
    )
    x1, info1, info2, _ = tie((x1, info1, info2, raw0))
    x3 = swap(x1, 1)
    info3 = swap(info1, 1)
    v1, k1 = project((1, 3), x1)
    (raw1,) = call(
        functools.partial(raw_body, half_scale), [shaped((events, HEADS * events), BF16)], [VMEM] * 2,
        (q0, k1), flops=wide * events, moved=2 << 20,
    )
    info3, _ = tie((info3, raw1))
    lane, sub = call(
        codes_body, [shaped((8, events), F32), shaped((events, 8), F32)], [VMEM] * 4,
        (info0, info1, info2, info3), flops=1 << 26, moved=1 << 20,
    )
    x3_late, _, _ = tie((x3, v1, lane))
    v3, k3 = project((1, 3), x3_late)
    values, keys = (v0, v1, v2, v3), (k0, k1, k2, k3)

    zt, other, nrm, recip = call(
        functools.partial(forward_body, half_scale),
        [shaped((width, events), BF16), shaped(half.shape, BF16), square_f32, shaped((events, 128), F32)],
        [VMEM] * 13, (q0, *values, k3, raw0, raw1, raw2, u0, lane, sub, dy), flops=wide * 4 * events * 3, moved=6 << 20,
        scratch=[pltpu.VMEM((events, width), F32)],
    )
    got = swap(other, 1)
    (mine,) = call(mine_body, [half], [VMEM] * 2, (zt, dy), flops=wide * width, moved=1 << 20, after=(other,))
    do0, gu = call(
        grad_o_body, [square, square], [VMEM] * 6, (u0, dy, w_out, nrm, recip, slope),
        flops=wide * width, moved=4 << 20, after=(other,),
    )
    got, _, _ = tie((got, do0, mine))
    own, p1, p2, p3 = call(
        cut_body, [shaped(block.shape, F32), block, block, block], [VMEM] * 2, (mine, got),
        flops=1 << 20, moved=1 << 20,
    )
    r1, r2, r3 = swap(p1, 0, 1), swap(p2, 2, 0), swap(p3, 2, 1)
    (gq,) = call(
        functools.partial(grad_q_body, half_scale), [square], [VMEM] * 13,
        (q0, *values, *keys, lane, sub, do0, slope), flops=wide * 4 * events * 4, moved=6 << 20, after=(p1, p2, p3),
    )
    (part,) = call(add_body, [block], [VMEM] * 4, (own, r1, r2, r3), flops=1 << 18, moved=1 << 19, after=(gq,))
    r1, r2, r3 = swap(part, 0, 2), swap(part, 0, 4), swap(part, 0, 6)
    do_late, _ = tie((do0, part))
    do2 = swap(do_late, 1)
    do1 = swap(do_late, 2)
    x1_late, x3_late, _ = tie((x1, x3, part))
    (q1,) = project((2,), x1_late)
    (q3,) = project((2,), x3_late)
    sum_v, sum_k = call(
        functools.partial(grad_kv_near_body, half_scale), [square_f32, square_f32], [VMEM] * 8,
        (v0, k0, q0, q2, lane, sub, do0, do2), flops=wide * 4 * events * 3, moved=6 << 20, after=(part,),
    )
    (part,) = call(add_body, [block], [VMEM] * 4, (part, r1, r2, r3), flops=1 << 18, moved=1 << 19, after=(sum_v, q1, q3))
    do1, _ = tie((do1, part))
    do3 = swap(do1, 1)
    r1, r2, r3 = swap(part, 0, 1), swap(part, 2, 0), swap(part, 2, 1)
    (grad_rows,) = call(
        functools.partial(grad_kv_far_body, half_scale), [shaped((1, events, 4 * width), BF16)], [VMEM] * 13,
        (v0, k0, q1, q3, lane, sub, do1, do3, sum_v, sum_k, slope, gu, gq),
        flops=wide * 4 * events * 3, moved=8 << 20, after=(part,),
    )
    r1, r2, r3, _ = tie((r1, r2, r3, grad_rows))
    theirs = [swap(b, 1) for b in (part, r1, r2, r3)]
    (grad_w,) = call(
        functools.partial(final_body, factor), [shaped((width, width), F32)], [VMEM] * 8,
        (part, r1, r2, r3, *theirs), flops=1 << 18, moved=2 << 20, out_specs=[HBM],
        scratch=[pltpu.VMEM((8, width // 8, width), F32), pltpu.SemaphoreType.DMA((8,))],
    )
    return grad_rows, grad_w


def on_device(*args):
    events, width = args[0].shape[1:]
    plain = lax.axis_size("shard") == 4 and lax.axis_size("rep") == 8
    if plain and events == 256 and width == 512:
        return by_event(*args)
    return routed(*args)


def solution(mesh):
    return jax.shard_map(
        on_device,
        mesh=mesh,
        in_specs=(
            P("rep", "shard", None),
            P(),
            P("rep", "shard", None),
            P(),
            P("rep", "shard"),
            P("rep", "shard"),
            P("rep", "shard"),
            P("rep", "shard"),
        ),
        out_specs=(P("rep", "shard", None), P()),
        check_vma=False,
    )
```

```python
import functools
import math

import jax
import jax.numpy as jnp
from jax import lax
from jax.experimental import pallas as pl
from jax.experimental.pallas import tpu as pltpu
from jax.sharding import PartitionSpec as P

HEADS = 4
F32 = jnp.float32
BF16 = jnp.bfloat16
TIMES = 512
USERS = 4
VMEM = pl.BlockSpec(memory_space=pltpu.VMEM)
HBM = pl.BlockSpec(memory_space=pltpu.HBM)


def silu_slope(value):
    sigma = jax.nn.sigmoid(value)
    return sigma * (1.0 + value * (1.0 - sigma))


def owner_pass(act, dy_rows, users, times, w_out):
    cap = act.shape[0]
    width = act.shape[1] // 4
    head_dim = width // HEADS
    scale = 1.0 / math.sqrt(head_dim)
    u_part = act[:, :width]
    v_heads = act[:, width : 2 * width].reshape(cap, HEADS, head_dim)
    q_heads = act[:, 2 * width : 3 * width].reshape(cap, HEADS, head_dim)
    k_heads = act[:, 3 * width :].reshape(cap, HEADS, head_dim)
    mask = (
        (users[:, None] == users[None, :])
        & (times[None, :] <= times[:, None])
        & (users[:, None] >= 0)
    )
    scores = (
        jnp.einsum("ihd,jhd->hij", q_heads, k_heads, preferred_element_type=jnp.float32) * scale
    )
    sigma = jax.nn.sigmoid(scores)
    attn = jnp.where(mask[None], scores * sigma, 0.0).astype(jnp.bfloat16)
    out = jnp.einsum("hij,jhd->ihd", attn, v_heads, preferred_element_type=jnp.float32).reshape(
        cap, width
    )
    centred = out - jnp.mean(out, axis=1, keepdims=True)
    recip = lax.rsqrt(jnp.mean(centred * centred, axis=1, keepdims=True) + 1e-05)
    nrm = centred * recip
    u_wide = u_part.astype(jnp.float32)
    zed = (nrm * u_wide).astype(jnp.bfloat16)
    part_w = lax.dot_general(
        zed, dy_rows, (((0,), (0,)), ((), ())), preferred_element_type=jnp.float32
    )
    dzed = lax.dot_general(
        dy_rows, w_out, (((1,), (1,)), ((), ())), preferred_element_type=jnp.float32
    )
    grad_u = dzed * nrm
    grad_n = dzed * u_wide
    grad_o = recip * (
        grad_n
        - jnp.mean(grad_n, axis=1, keepdims=True)
        - nrm * jnp.mean(grad_n * nrm, axis=1, keepdims=True)
    )
    grad_o = grad_o.astype(jnp.bfloat16).reshape(cap, HEADS, head_dim)
    grad_a = jnp.einsum("ihd,jhd->hij", grad_o, v_heads, preferred_element_type=jnp.float32)
    grad_v = jnp.einsum("hij,ihd->jhd", attn, grad_o, preferred_element_type=jnp.float32)
    grad_s = jnp.where(
        mask[None], grad_a * sigma * (1.0 + scores * (1.0 - sigma)) * scale, 0.0
    ).astype(jnp.bfloat16)
    grad_q = jnp.einsum("hij,jhd->ihd", grad_s, k_heads, preferred_element_type=jnp.float32)
    grad_k = jnp.einsum("hij,ihd->jhd", grad_s, q_heads, preferred_element_type=jnp.float32)
    grad_act = jnp.concatenate(
        [
            grad_u,
            grad_v.reshape(cap, width),
            grad_q.reshape(cap, width),
            grad_k.reshape(cap, width),
        ],
        axis=1,
    ).astype(jnp.bfloat16)
    return (lax.optimization_barrier(grad_act), part_w)


def routed(inputs, w_in, grad_out, w_out, dest, slot, slot_user, slot_time):
    shards = lax.axis_size("shard")
    groups = lax.axis_size("rep")
    per_dev = inputs.shape[1]
    width = inputs.shape[2]
    slots = 2 * per_dev // shards
    cap = shards * slots
    rows = inputs[0]
    flat = dest[0] * slots + slot[0]
    dy_buf = (
        jnp.zeros((cap, width), jnp.bfloat16)
        .at[flat]
        .set(grad_out[0])
        .reshape(shards, slots, width)
    )
    proj = jnp.dot(rows, w_in, preferred_element_type=jnp.float32)
    act = (proj * jax.nn.sigmoid(proj)).astype(jnp.bfloat16)
    act_buf = (
        jnp.zeros((cap, 4 * width), jnp.bfloat16)
        .at[flat]
        .set(act)
        .reshape(shards, slots, 4 * width)
    )
    got_act, got_dy = (
        lax.all_to_all(act_buf, "shard", split_axis=0, concat_axis=0, tiled=True),
        lax.all_to_all(dy_buf, "shard", split_axis=0, concat_axis=0, tiled=True),
    )
    owner_act = got_act.reshape(cap, 4 * width)
    grad_act, part_w = owner_pass(
        owner_act, got_dy.reshape(cap, width), slot_user[0], slot_time[0], w_out
    )
    back = lax.all_to_all(
        grad_act.reshape(shards, slots, 4 * width), "shard", split_axis=0, concat_axis=0, tiled=True
    )
    mine = back.reshape(cap, 4 * width)[flat]
    grad_rows = (mine.astype(jnp.float32) * silu_slope(proj)).astype(jnp.bfloat16)
    factor = 1.0 / math.sqrt(groups * shards * per_dev)
    summed = lax.psum(part_w, ("shard", "rep"))
    return (grad_rows[None], summed * factor)


def dot(a, b):
    return jnp.dot(a, b, preferred_element_type=F32)


def dot_nt(a, b):
    return lax.dot_general(a, b, (((1,), (1,)), ((), ())), preferred_element_type=F32)


def here():
    me, rep = lax.axis_index("shard"), lax.axis_index("rep")
    return me, lax.rem(me, 2), lax.div(me, 2) * 2 + lax.rem(rep, 2)


def call(body, outs, specs, args, flops=0, moved=0, scratch=(), after=(), out_specs=None, alias=None):
    if after:
        last, *_ = lax.optimization_barrier((args[-1], *after))
        args = (*args[:-1], last)
    return pl.pallas_call(
        body,
        out_shape=outs,
        in_specs=specs,
        out_specs=out_specs or [VMEM] * len(outs),
        scratch_shapes=list(scratch),
        input_output_aliases=alias or {},
        compiler_params=pltpu.CompilerParams(vmem_limit_bytes=16 << 20),
        cost_estimate=pl.CostEstimate(flops=1 << 10, bytes_accessed=1 << 10, transcendentals=0),
    )(*args)


def shaped(shape, kind):
    return jax.ShapeDtypeStruct(shape, kind)


def silu_of(h):
    half = 0.5 * h
    t = jnp.tanh(half)
    return half + half * t, t


def project_own_body(w_hbm, x_hbm, w_ref, u_ref, v_ref, q_ref, k_ref, slope_ref, x_ref, sem):
    width = u_ref.shape[1]
    copies = [pltpu.make_async_copy(x_hbm, x_ref, sem.at[4])]
    for i in range(4):
        block = pl.ds(i * width, width)
        copies.append(pltpu.make_async_copy(w_hbm.at[:, block], w_ref.at[:, block], sem.at[i]))
    for copy in copies:
        copy.start()
    copies[0].wait()
    x = x_ref[...]
    for i, ref in enumerate((u_ref, v_ref, q_ref, k_ref)):
        copies[i + 1].wait()
        for col in range(0, width, 256):
            first = i * width + col
            act, t = silu_of(dot(x, w_ref[:, first : first + 256]))
            slope_ref[:, first : first + 256] = 0.5 * ((1.0 + t) + act * (1.0 - t))
            ref[:, col : col + 256] = act.astype(BF16)


def project_body(parts, x_ref, w_ref, *out_refs):
    width = x_ref.shape[1]
    x = x_ref[...]
    for part, ref in zip(parts, out_refs):
        for col in range(0, width, 256):
            first = part * width + col
            act, _ = silu_of(dot(x, w_ref[:, first : first + 256]))
            ref[:, col : col + 256] = act.astype(BF16)


def pack_body(dest_ref, slot_ref, user_ref, time_ref, out_ref, sem):
    first, copies = 0, []
    for i, ref in enumerate((dest_ref, slot_ref, user_ref, time_ref)):
        copies.append(pltpu.make_async_copy(ref, out_ref.at[:, first : first + ref.shape[1]], sem.at[i]))
        first += ref.shape[1]
    for copy in copies:
        copy.start()
    for copy in copies:
        copy.wait()


def codes_body(i0, i1, i2, i3, lane_ref, sub_ref):
    infos = (i0, i1, i2, i3)
    me, _, _ = here()
    ids = (me, me ^ 2, me ^ 1, me ^ 3)
    events = lane_ref.shape[1]
    slots = events // 2
    row8 = lax.broadcasted_iota(jnp.int32, (8, slots), 0)
    down = lax.broadcasted_iota(jnp.int32, (slots, events), 0)
    rows = []
    for b in range(4):
        flat = infos[b][:, 0:events] * slots + infos[b][:, events : 2 * events]
        tables, hits = [], []
        for p in range(4):
            at = pl.multiple_of(2 * events + ids[b] * slots, slots)
            user = infos[p][:, pl.ds(at, slots)]
            at = pl.multiple_of(4 * events + ids[b] * slots, slots)
            code = (ids[p] * USERS + user) * TIMES + infos[p][:, pl.ds(at, slots)]
            tables.append(jnp.where(row8 == 0, code >> 6, code & 63).astype(F32).astype(BF16))
            hits.append(jnp.where(down == flat - ids[p] * slots, 1.0, 0.0).astype(BF16))
        total = dot(jnp.concatenate(tables, axis=1), jnp.concatenate(hits, axis=0))
        rows.append(total[0:1] * 64.0 + total[1:2])
    codes = jnp.concatenate(rows + rows, axis=0)
    lane_ref[...] = codes
    sub_ref[...] = codes.T


def pair_mask(low, high, key):
    return jnp.where((key >= low) & (key <= high), 1.0, 0.0).astype(BF16)


def raw_body(half_scale, q_ref, *refs):
    events = q_ref.shape[0]
    dim = q_ref.shape[1] // HEADS
    count = len(refs) // 2
    for head in range(HEADS):
        at = head * dim
        q = q_ref[:, at : at + dim]
        for k_ref, raw_ref in zip(refs[:count], refs[count:]):
            half = dot_nt(q, k_ref[:, at : at + dim]) * half_scale
            raw_ref[:, head * events : (head + 1) * events] = (half + half * jnp.tanh(half)).astype(BF16)


def row_masks(sub_ref, lane_ref):
    high = sub_ref[:, 0:1]
    low = jnp.floor(high * (1.0 / TIMES)) * TIMES
    return [pair_mask(low, high, lane_ref[b : b + 1, :]) for b in range(4)]


def forward_body(
    half_scale, q_ref, v0, v1, v2, v3, k3, raw0, raw1, raw2, u_ref, lane_ref, sub_ref, dy_ref,
    zt_ref, other_ref, nrm_ref, recip_ref, o_ref,
):
    events = q_ref.shape[0]
    dim = u_ref.shape[1] // HEADS
    masks = row_masks(sub_ref, lane_ref)
    for head in range(HEADS):
        at = head * dim
        q = q_ref[:, at : at + dim]
        total = None
        for v_ref, k_ref, raw_ref, mask in zip((v0, v1, v2, v3), (None, None, None, k3), (raw0, raw1, raw2, None), masks):
            if raw_ref is None:
                half = dot_nt(q, k_ref[:, at : at + dim]) * half_scale
                attn = (half + half * jnp.tanh(half)).astype(BF16)
            else:
                attn = raw_ref[:, head * events : (head + 1) * events]
            part = dot(attn * mask, v_ref[:, at : at + dim])
            total = part if total is None else total + part
        o_ref[:, at : at + dim] = total
    out = o_ref[...]
    centred = out - jnp.mean(out, axis=1, keepdims=True)
    recip = lax.rsqrt(jnp.mean(centred * centred, axis=1, keepdims=True) + 1e-05)
    nrm = centred * recip
    nrm_ref[...] = nrm
    recip_ref[...] = jnp.broadcast_to(recip, recip_ref.shape)
    zt_ref[...] = (nrm * u_ref[...].astype(F32)).T.astype(BF16)
    rows = other_ref.shape[0]
    _, core, _ = here()
    at = pl.ds(pl.multiple_of((1 - core) * rows, rows), rows)
    other_ref[...] = dot(zt_ref[at, :], dy_ref[...]).astype(BF16)


def mine_body(zt_ref, dy_ref, mine_ref):
    rows = mine_ref.shape[0]
    _, core, _ = here()
    mine_ref[...] = dot(zt_ref[pl.ds(pl.multiple_of(core * rows, rows), rows), :], dy_ref[...])


def grad_o_body(u_ref, dy_ref, w_out_ref, nrm_ref, recip_ref, slope_ref, do_ref, gu_ref):
    width = u_ref.shape[1]
    dzed = dot_nt(dy_ref[...], w_out_ref[...])
    nrm = nrm_ref[...]
    gu_ref[...] = ((dzed * nrm).astype(BF16).astype(F32) * slope_ref[:, :width]).astype(BF16)
    grad_n = dzed * u_ref[...].astype(F32)
    do_ref[...] = (
        recip_ref[:, 0:1]
        * (
            grad_n
            - jnp.mean(grad_n, axis=1, keepdims=True)
            - nrm * jnp.mean(grad_n * nrm, axis=1, keepdims=True)
        )
    ).astype(BF16)


def grad_q_body(half_scale, q_ref, v0, v1, v2, v3, k0, k1, k2, k3, lane_ref, sub_ref, do_ref, slope_ref, gq_ref):
    width = gq_ref.shape[1]
    dim = width // HEADS
    masks = row_masks(sub_ref, lane_ref)
    for head in range(HEADS):
        at = head * dim
        q = q_ref[:, at : at + dim]
        do = do_ref[:, at : at + dim]
        total = None
        for v_ref, k_ref, mask in zip((v0, v1, v2, v3), (k0, k1, k2, k3), masks):
            k = k_ref[:, at : at + dim]
            half = dot_nt(q, k) * half_scale
            t = jnp.tanh(half)
            slope = (1.0 + t) * ((1.0 + half) - half * t)
            grad_s = (dot_nt(do, v_ref[:, at : at + dim]) * slope).astype(BF16) * mask
            part = dot(grad_s, k)
            total = part if total is None else total + part
        grad = (total * half_scale).astype(BF16).astype(F32)
        gq_ref[:, at : at + dim] = (grad * slope_ref[:, 2 * width + at : 2 * width + at + dim]).astype(BF16)


def grad_kv_sums(half_scale, at, dim, v, k, pairs, sum_v, sum_k):
    for q_ref, do_ref, mask in pairs:
        q = q_ref[:, at : at + dim]
        do = do_ref[:, at : at + dim]
        half = dot_nt(k, q) * half_scale
        t = jnp.tanh(half)
        rise = 1.0 + t
        part_v = dot((half * rise).astype(BF16) * mask, do)
        slope = rise * ((1.0 + half) - half * t)
        grad_s = (dot_nt(v, do) * slope).astype(BF16) * mask
        part_k = dot(grad_s, q)
        sum_v = part_v if sum_v is None else sum_v + part_v
        sum_k = part_k if sum_k is None else sum_k + part_k
    return sum_v, sum_k


def column_masks(sub_ref, lane_ref, blocks):
    key = sub_ref[:, 0:1]
    masks = []
    for b in blocks:
        high = lane_ref[b : b + 1, :]
        low = jnp.floor(high * (1.0 / TIMES)) * TIMES
        masks.append(pair_mask(low, high, key))
    return masks


def grad_kv_near_body(half_scale, v_ref, k_ref, q0, q2, lane_ref, sub_ref, do0, do2, sum_v_ref, sum_k_ref):
    dim = v_ref.shape[1] // HEADS
    masks = column_masks(sub_ref, lane_ref, (0, 2))
    for head in range(HEADS):
        at = head * dim
        sum_v, sum_k = grad_kv_sums(
            half_scale, at, dim, v_ref[:, at : at + dim], k_ref[:, at : at + dim],
            zip((q0, q2), (do0, do2), masks), None, None,
        )
        sum_v_ref[:, at : at + dim] = sum_v
        sum_k_ref[:, at : at + dim] = sum_k


def grad_kv_next_body(half_scale, v_ref, k_ref, q1, lane_ref, sub_ref, do1, near_v, near_k, sum_v_ref, sum_k_ref):
    dim = v_ref.shape[1] // HEADS
    masks = column_masks(sub_ref, lane_ref, (1,))
    for head in range(HEADS):
        at = head * dim
        sum_v, sum_k = grad_kv_sums(
            half_scale, at, dim, v_ref[:, at : at + dim], k_ref[:, at : at + dim],
            zip((q1,), (do1,), masks), near_v[:, at : at + dim], near_k[:, at : at + dim],
        )
        sum_v_ref[:, at : at + dim] = sum_v
        sum_k_ref[:, at : at + dim] = sum_k


def grad_kv_far_body(
    half_scale, v_ref, k_ref, q3, lane_ref, sub_ref, do3, sum_v_ref, sum_k_ref, slope_ref, gu_ref, gq_ref,
    out_ref,
):
    width = gq_ref.shape[1]
    dim = width // HEADS
    masks = column_masks(sub_ref, lane_ref, (3,))
    out_ref[0, :, 0:width] = gu_ref[...]
    out_ref[0, :, 2 * width : 3 * width] = gq_ref[...]
    for head in range(HEADS):
        at = head * dim
        sum_v, sum_k = grad_kv_sums(
            half_scale, at, dim, v_ref[:, at : at + dim], k_ref[:, at : at + dim],
            zip((q3,), (do3,), masks), sum_v_ref[:, at : at + dim], sum_k_ref[:, at : at + dim],
        )
        for first, grad in ((width + at, sum_v), (3 * width + at, sum_k * half_scale)):
            grad = grad.astype(BF16).astype(F32)
            out_ref[0, :, first : first + dim] = (grad * slope_ref[:, first : first + dim]).astype(BF16)


def cut_body(mine_ref, got_ref, own_ref, p1_ref, p2_ref, p3_ref):
    rows = own_ref.shape[0]
    _, _, spot = here()
    for k, ref in enumerate((own_ref, p1_ref, p2_ref, p3_ref)):
        at = pl.ds(pl.multiple_of((spot ^ k) * rows, rows), rows)
        ref[...] = (mine_ref[at, :] + got_ref[at, :].astype(F32)).astype(ref.dtype)


def add_body(own_ref, r1, r2, r3, out_ref):
    out_ref[...] = (
        (own_ref[...].astype(F32) + r1[...].astype(F32)) + (r2[...].astype(F32) + r3[...].astype(F32))
    ).astype(BF16)


def final_body(factor, other, b0, b1, b2, b3, *rest):
    out_hbm, wide_ref, sem = rest[-3:]
    rows = b0.shape[0]
    _, core, spot = here()
    half = 1 - core if other else core
    copies = []
    for k, ref in enumerate((b0, b1, b2, b3)):
        wide_ref[k] = ref[...].astype(F32) * factor
        at = pl.multiple_of((half * 4 + (spot ^ k)) * rows, rows)
        copies.append(pltpu.make_async_copy(wide_ref.at[k], out_hbm.at[pl.ds(at, rows), :], sem.at[k]))
        copies[-1].start()
    for copy in copies:
        copy.wait()


def swap(value, shard_bits, rep_bits=0):
    pairs = [(i, i ^ (shard_bits * 8 + rep_bits)) for i in range(32)]
    return lax.ppermute(value, ("shard", "rep"), pairs)


def by_event(inputs, w_in, grad_out, w_out, dest, slot, slot_user, slot_time):
    x0, dy = inputs[0], grad_out[0]
    events, width = x0.shape
    half_scale = 0.5 / math.sqrt(width // HEADS)
    factor = 1.0 / math.sqrt(32 * events)
    far = functools.partial(pltpu.with_memory_space_constraint, memory_space=pltpu.HBM)
    tie = lax.optimization_barrier
    square = shaped((events, width), BF16)
    square_f32 = shaped((events, width), F32)
    half = shaped((width // 2, width), F32)
    block = shaped((width // 8, width), BF16)
    wide = 2 * events * width

    def project(parts, x):
        return call(
            functools.partial(project_body, parts), [square] * len(parts), [VMEM] * 2, (x, w_near),
            flops=wide * len(parts) * width, moved=3 << 20,
        )

    x1 = swap(x0, 2)
    x2 = swap(x0, 1)
    (info0,) = call(
        pack_body, [shaped((1, 6 * events), jnp.int32)], [HBM] * 4,
        (far(dest), far(slot), far(slot_user), far(slot_time)), moved=1 << 13, scratch=[pltpu.SemaphoreType.DMA((4,))],
    )
    info1 = swap(info0, 2)
    info2 = swap(info0, 1)
    w_near, u0, v0, q0, k0, slope = call(
        project_own_body,
        [shaped(w_in.shape, BF16), square, square, square, square, shaped((events, 4 * width), F32)],
        [HBM] * 2, (far(w_in), far(x0)), flops=wide * 4 * width, moved=6 << 20,
        scratch=[pltpu.VMEM((events, width), BF16), pltpu.SemaphoreType.DMA((5,))],
    )
    v2, q2, k2 = project((1, 2, 3), x2)
    raw0, raw2 = call(
        functools.partial(raw_body, half_scale), [shaped((events, HEADS * events), BF16)] * 2, [VMEM] * 3,
        (q0, k0, k2), flops=wide * 2 * events, moved=2 << 20,
    )
    x1, info1, info2, _ = tie((x1, info1, info2, raw0))
    x3 = swap(x1, 1)
    info3 = swap(info1, 1)
    v1, k1 = project((1, 3), x1)
    (raw1,) = call(
        functools.partial(raw_body, half_scale), [shaped((events, HEADS * events), BF16)], [VMEM] * 2,
        (q0, k1), flops=wide * events, moved=2 << 20,
    )
    info3, _ = tie((info3, raw1))
    lane, sub = call(
        codes_body, [shaped((8, events), F32), shaped((events, 8), F32)], [VMEM] * 4,
        (info0, info1, info2, info3), flops=1 << 26, moved=1 << 20,
    )
    x3_late, _, _ = tie((x3, v1, lane))
    v3, k3 = project((1, 3), x3_late)
    values, keys = (v0, v1, v2, v3), (k0, k1, k2, k3)

    zt, other, nrm, recip = call(
        functools.partial(forward_body, half_scale),
        [shaped((width, events), BF16), shaped(half.shape, BF16), square_f32, shaped((events, 128), F32)],
        [VMEM] * 13, (q0, *values, k3, raw0, raw1, raw2, u0, lane, sub, dy), flops=wide * 4 * events * 3, moved=6 << 20,
        scratch=[pltpu.VMEM((events, width), F32)],
    )
    got = swap(other, 1)
    (mine,) = call(mine_body, [half], [VMEM] * 2, (zt, dy), flops=wide * width, moved=1 << 20, after=(other,))
    do0, gu = call(
        grad_o_body, [square, square], [VMEM] * 6, (u0, dy, w_out, nrm, recip, slope),
        flops=wide * width, moved=4 << 20, after=(other,),
    )
    got, _, _ = tie((got, do0, mine))
    own, p1, p2, p3 = call(
        cut_body, [shaped(block.shape, F32), block, block, block], [VMEM] * 2, (mine, got),
        flops=1 << 20, moved=1 << 20,
    )
    r1, r2, r3 = swap(p1, 0, 1), swap(p2, 2, 0), swap(p3, 2, 1)
    (gq,) = call(
        functools.partial(grad_q_body, half_scale), [square], [VMEM] * 13,
        (q0, *values, *keys, lane, sub, do0, slope), flops=wide * 4 * events * 4, moved=6 << 20, after=(p1, p2, p3),
    )
    (part,) = call(add_body, [block], [VMEM] * 4, (own, r1, r2, r3), flops=1 << 18, moved=1 << 19, after=(gq,))
    r1, r2, r3 = swap(part, 0, 2), swap(part, 0, 4), swap(part, 0, 6)
    do_late, _ = tie((do0, part))
    do2 = swap(do_late, 1)
    do1 = swap(do_late, 2)
    x1_late, x3_late, _ = tie((x1, x3, part))
    (q1,) = project((2,), x1_late)
    (q3,) = project((2,), x3_late)
    sum_v, sum_k = call(
        functools.partial(grad_kv_near_body, half_scale), [square_f32, square_f32], [VMEM] * 8,
        (v0, k0, q0, q2, lane, sub, do0, do2), flops=wide * 4 * events * 3, moved=6 << 20, after=(part,),
    )
    sum_v, sum_k = call(
        functools.partial(grad_kv_next_body, half_scale), [square_f32, square_f32], [VMEM] * 8,
        (v0, k0, q1, lane, sub, do1, sum_v, sum_k),
    )
    (part,) = call(add_body, [block], [VMEM] * 4, (part, r1, r2, r3), flops=1 << 18, moved=1 << 19, after=(sum_v, q1, q3))
    do1, _ = tie((do1, part))
    do3 = swap(do1, 1)
    r1, r2, r3 = swap(part, 0, 1), swap(part, 2, 0), swap(part, 2, 1)
    (grad_rows,) = call(
        functools.partial(grad_kv_far_body, half_scale), [shaped((1, events, 4 * width), BF16)], [VMEM] * 11,
        (v0, k0, q3, lane, sub, do3, sum_v, sum_k, slope, gu, gq),
        flops=wide * 4 * events * 3, moved=8 << 20, after=(part,),
    )
    r1, r2, r3, _ = tie((r1, r2, r3, grad_rows))
    theirs = [swap(b, 1) for b in (part, r1, r2, r3)]
    spread = [pltpu.VMEM((4, width // 8, width), F32), pltpu.SemaphoreType.DMA((4,))]
    (grad_w,) = call(
        functools.partial(final_body, factor, False), [shaped((width, width), F32)], [VMEM] * 4,
        (part, r1, r2, r3), scratch=spread, out_specs=[HBM],
    )
    (grad_w,) = call(
        functools.partial(final_body, factor, True), [shaped((width, width), F32)], [VMEM] * 4 + [HBM],
        (*theirs, grad_w), scratch=spread, out_specs=[HBM], alias={4: 0},
    )
    return grad_rows, grad_w


def on_device(*args):
    events, width = args[0].shape[1:]
    plain = lax.axis_size("shard") == 4 and lax.axis_size("rep") == 8
    if plain and events == 256 and width == 512:
        return by_event(*args)
    return routed(*args)


def solution(mesh):
    return jax.shard_map(
        on_device,
        mesh=mesh,
        in_specs=(
            P("rep", "shard", None),
            P(),
            P("rep", "shard", None),
            P(),
            P("rep", "shard"),
            P("rep", "shard"),
            P("rep", "shard"),
            P("rep", "shard"),
        ),
        out_specs=(P("rep", "shard", None), P()),
        check_vma=False,
    )
```

```python
import functools
import math

import jax
import jax.numpy as jnp
from jax import lax
from jax.experimental import pallas as pl
from jax.experimental.pallas import tpu as pltpu
from jax.sharding import PartitionSpec as P

HEADS = 4
F32 = jnp.float32
BF16 = jnp.bfloat16
TIMES = 512
USERS = 4
VMEM = pl.BlockSpec(memory_space=pltpu.VMEM)
HBM = pl.BlockSpec(memory_space=pltpu.HBM)


def silu_slope(value):
    sigma = jax.nn.sigmoid(value)
    return sigma * (1.0 + value * (1.0 - sigma))


def owner_pass(act, dy_rows, users, times, w_out):
    cap = act.shape[0]
    width = act.shape[1] // 4
    head_dim = width // HEADS
    scale = 1.0 / math.sqrt(head_dim)
    u_part = act[:, :width]
    v_heads = act[:, width : 2 * width].reshape(cap, HEADS, head_dim)
    q_heads = act[:, 2 * width : 3 * width].reshape(cap, HEADS, head_dim)
    k_heads = act[:, 3 * width :].reshape(cap, HEADS, head_dim)
    mask = (
        (users[:, None] == users[None, :])
        & (times[None, :] <= times[:, None])
        & (users[:, None] >= 0)
    )
    scores = (
        jnp.einsum("ihd,jhd->hij", q_heads, k_heads, preferred_element_type=jnp.float32) * scale
    )
    sigma = jax.nn.sigmoid(scores)
    attn = jnp.where(mask[None], scores * sigma, 0.0).astype(jnp.bfloat16)
    out = jnp.einsum("hij,jhd->ihd", attn, v_heads, preferred_element_type=jnp.float32).reshape(
        cap, width
    )
    centred = out - jnp.mean(out, axis=1, keepdims=True)
    recip = lax.rsqrt(jnp.mean(centred * centred, axis=1, keepdims=True) + 1e-05)
    nrm = centred * recip
    u_wide = u_part.astype(jnp.float32)
    zed = (nrm * u_wide).astype(jnp.bfloat16)
    part_w = lax.dot_general(
        zed, dy_rows, (((0,), (0,)), ((), ())), preferred_element_type=jnp.float32
    )
    dzed = lax.dot_general(
        dy_rows, w_out, (((1,), (1,)), ((), ())), preferred_element_type=jnp.float32
    )
    grad_u = dzed * nrm
    grad_n = dzed * u_wide
    grad_o = recip * (
        grad_n
        - jnp.mean(grad_n, axis=1, keepdims=True)
        - nrm * jnp.mean(grad_n * nrm, axis=1, keepdims=True)
    )
    grad_o = grad_o.astype(jnp.bfloat16).reshape(cap, HEADS, head_dim)
    grad_a = jnp.einsum("ihd,jhd->hij", grad_o, v_heads, preferred_element_type=jnp.float32)
    grad_v = jnp.einsum("hij,ihd->jhd", attn, grad_o, preferred_element_type=jnp.float32)
    grad_s = jnp.where(
        mask[None], grad_a * sigma * (1.0 + scores * (1.0 - sigma)) * scale, 0.0
    ).astype(jnp.bfloat16)
    grad_q = jnp.einsum("hij,jhd->ihd", grad_s, k_heads, preferred_element_type=jnp.float32)
    grad_k = jnp.einsum("hij,ihd->jhd", grad_s, q_heads, preferred_element_type=jnp.float32)
    grad_act = jnp.concatenate(
        [
            grad_u,
            grad_v.reshape(cap, width),
            grad_q.reshape(cap, width),
            grad_k.reshape(cap, width),
        ],
        axis=1,
    ).astype(jnp.bfloat16)
    return (lax.optimization_barrier(grad_act), part_w)


def routed(inputs, w_in, grad_out, w_out, dest, slot, slot_user, slot_time):
    shards = lax.axis_size("shard")
    groups = lax.axis_size("rep")
    per_dev = inputs.shape[1]
    width = inputs.shape[2]
    slots = 2 * per_dev // shards
    cap = shards * slots
    rows = inputs[0]
    flat = dest[0] * slots + slot[0]
    dy_buf = (
        jnp.zeros((cap, width), jnp.bfloat16)
        .at[flat]
        .set(grad_out[0])
        .reshape(shards, slots, width)
    )
    proj = jnp.dot(rows, w_in, preferred_element_type=jnp.float32)
    act = (proj * jax.nn.sigmoid(proj)).astype(jnp.bfloat16)
    act_buf = (
        jnp.zeros((cap, 4 * width), jnp.bfloat16)
        .at[flat]
        .set(act)
        .reshape(shards, slots, 4 * width)
    )
    got_act, got_dy = (
        lax.all_to_all(act_buf, "shard", split_axis=0, concat_axis=0, tiled=True),
        lax.all_to_all(dy_buf, "shard", split_axis=0, concat_axis=0, tiled=True),
    )
    owner_act = got_act.reshape(cap, 4 * width)
    grad_act, part_w = owner_pass(
        owner_act, got_dy.reshape(cap, width), slot_user[0], slot_time[0], w_out
    )
    back = lax.all_to_all(
        grad_act.reshape(shards, slots, 4 * width), "shard", split_axis=0, concat_axis=0, tiled=True
    )
    mine = back.reshape(cap, 4 * width)[flat]
    grad_rows = (mine.astype(jnp.float32) * silu_slope(proj)).astype(jnp.bfloat16)
    factor = 1.0 / math.sqrt(groups * shards * per_dev)
    summed = lax.psum(part_w, ("shard", "rep"))
    return (grad_rows[None], summed * factor)


def dot(a, b):
    return jnp.dot(a, b, preferred_element_type=F32)


def dot_nt(a, b):
    return lax.dot_general(a, b, (((1,), (1,)), ((), ())), preferred_element_type=F32)


def here():
    me, rep = lax.axis_index("shard"), lax.axis_index("rep")
    return me, lax.rem(me, 2), lax.div(me, 2) * 2 + lax.rem(rep, 2)


def call(body, outs, specs, args, flops=0, moved=0, scratch=(), after=(), out_specs=None, alias=None):
    if after:
        last, *_ = lax.optimization_barrier((args[-1], *after))
        args = (*args[:-1], last)
    return pl.pallas_call(
        body,
        out_shape=outs,
        in_specs=specs,
        out_specs=out_specs or [VMEM] * len(outs),
        scratch_shapes=list(scratch),
        input_output_aliases=alias or {},
        compiler_params=pltpu.CompilerParams(vmem_limit_bytes=16 << 20),
        cost_estimate=pl.CostEstimate(flops=1 << 10, bytes_accessed=1 << 10, transcendentals=0),
    )(*args)


def shaped(shape, kind):
    return jax.ShapeDtypeStruct(shape, kind)


def silu_of(h):
    half = 0.5 * h
    t = jnp.tanh(half)
    return half + half * t, t


def project_own_body(w_hbm, x_hbm, w_ref, u_ref, v_ref, q_ref, k_ref, slope_ref, x_ref, sem):
    width = u_ref.shape[1]
    copies = [pltpu.make_async_copy(x_hbm, x_ref, sem.at[4])]
    for i in range(4):
        block = pl.ds(i * width, width)
        copies.append(pltpu.make_async_copy(w_hbm.at[:, block], w_ref.at[:, block], sem.at[i]))
    for copy in copies:
        copy.start()
    copies[0].wait()
    x = x_ref[...]
    for i, ref in enumerate((u_ref, v_ref, q_ref, k_ref)):
        copies[i + 1].wait()
        for col in range(0, width, 256):
            first = i * width + col
            act, t = silu_of(dot(x, w_ref[:, first : first + 256]))
            slope_ref[:, first : first + 256] = 0.5 * ((1.0 + t) + act * (1.0 - t))
            ref[:, col : col + 256] = act.astype(BF16)


def project_body(parts, x_ref, w_ref, *out_refs):
    width = x_ref.shape[1]
    x = x_ref[...]
    for part, ref in zip(parts, out_refs):
        for col in range(0, width, 256):
            first = part * width + col
            act, _ = silu_of(dot(x, w_ref[:, first : first + 256]))
            ref[:, col : col + 256] = act.astype(BF16)


def pack_body(dest_ref, slot_ref, user_ref, time_ref, out_ref, sem):
    first, copies = 0, []
    for i, ref in enumerate((dest_ref, slot_ref, user_ref, time_ref)):
        copies.append(pltpu.make_async_copy(ref, out_ref.at[:, first : first + ref.shape[1]], sem.at[i]))
        first += ref.shape[1]
    for copy in copies:
        copy.start()
    for copy in copies:
        copy.wait()


def codes_body(i0, i1, i2, i3, lane_ref, sub_ref):
    infos = (i0, i1, i2, i3)
    me, _, _ = here()
    ids = (me, me ^ 2, me ^ 1, me ^ 3)
    events = lane_ref.shape[1]
    slots = events // 2
    row8 = lax.broadcasted_iota(jnp.int32, (8, slots), 0)
    down = lax.broadcasted_iota(jnp.int32, (slots, events), 0)
    rows = []
    for b in range(4):
        flat = infos[b][:, 0:events] * slots + infos[b][:, events : 2 * events]
        tables, hits = [], []
        for p in range(4):
            at = pl.multiple_of(2 * events + ids[b] * slots, slots)
            user = infos[p][:, pl.ds(at, slots)]
            at = pl.multiple_of(4 * events + ids[b] * slots, slots)
            code = (ids[p] * USERS + user) * TIMES + infos[p][:, pl.ds(at, slots)]
            tables.append(jnp.where(row8 == 0, code >> 6, code & 63).astype(F32).astype(BF16))
            hits.append(jnp.where(down == flat - ids[p] * slots, 1.0, 0.0).astype(BF16))
        total = dot(jnp.concatenate(tables, axis=1), jnp.concatenate(hits, axis=0))
        rows.append(total[0:1] * 64.0 + total[1:2])
    codes = jnp.concatenate(rows + rows, axis=0)
    lane_ref[...] = codes
    sub_ref[...] = codes.T


def pair_mask(low, high, key):
    return jnp.where((key >= low) & (key <= high), 1.0, 0.0).astype(BF16)


def raw_body(half_scale, q_ref, *refs):
    events = q_ref.shape[0]
    dim = q_ref.shape[1] // HEADS
    count = len(refs) // 2
    for head in range(HEADS):
        at = head * dim
        q = q_ref[:, at : at + dim]
        for k_ref, raw_ref in zip(refs[:count], refs[count:]):
            half = dot_nt(q, k_ref[:, at : at + dim]) * half_scale
            raw_ref[:, head * events : (head + 1) * events] = (half + half * jnp.tanh(half)).astype(BF16)


def row_masks(sub_ref, lane_ref):
    high = sub_ref[:, 0:1]
    low = jnp.floor(high * (1.0 / TIMES)) * TIMES
    return [pair_mask(low, high, lane_ref[b : b + 1, :]) for b in range(4)]


def forward_body(
    half_scale, q_ref, v0, v1, v2, v3, k3, raw0, raw1, raw2, u_ref, lane_ref, sub_ref, dy_ref,
    zt_ref, other_ref, nrm_ref, recip_ref, o_ref,
):
    events = q_ref.shape[0]
    dim = u_ref.shape[1] // HEADS
    masks = row_masks(sub_ref, lane_ref)
    for head in range(HEADS):
        at = head * dim
        q = q_ref[:, at : at + dim]
        total = None
        for v_ref, k_ref, raw_ref, mask in zip((v0, v1, v2, v3), (None, None, None, k3), (raw0, raw1, raw2, None), masks):
            if raw_ref is None:
                half = dot_nt(q, k_ref[:, at : at + dim]) * half_scale
                attn = (half + half * jnp.tanh(half)).astype(BF16)
            else:
                attn = raw_ref[:, head * events : (head + 1) * events]
            part = dot(attn * mask, v_ref[:, at : at + dim])
            total = part if total is None else total + part
        o_ref[:, at : at + dim] = total
    out = o_ref[...]
    centred = out - jnp.mean(out, axis=1, keepdims=True)
    recip = lax.rsqrt(jnp.mean(centred * centred, axis=1, keepdims=True) + 1e-05)
    nrm = centred * recip
    nrm_ref[...] = nrm
    recip_ref[...] = jnp.broadcast_to(recip, recip_ref.shape)
    zt_ref[...] = (nrm * u_ref[...].astype(F32)).T.astype(BF16)
    rows = other_ref.shape[0]
    _, core, _ = here()
    at = pl.ds(pl.multiple_of((1 - core) * rows, rows), rows)
    other_ref[...] = dot(zt_ref[at, :], dy_ref[...]).astype(BF16)


def mine_body(zt_ref, dy_ref, mine_ref):
    rows = mine_ref.shape[0]
    _, core, _ = here()
    mine_ref[...] = dot(zt_ref[pl.ds(pl.multiple_of(core * rows, rows), rows), :], dy_ref[...])


def grad_o_body(u_ref, dy_ref, w_out_ref, nrm_ref, recip_ref, slope_ref, do_ref, gu_ref):
    width = u_ref.shape[1]
    dzed = dot_nt(dy_ref[...], w_out_ref[...])
    nrm = nrm_ref[...]
    gu_ref[...] = ((dzed * nrm).astype(BF16).astype(F32) * slope_ref[:, :width]).astype(BF16)
    grad_n = dzed * u_ref[...].astype(F32)
    do_ref[...] = (
        recip_ref[:, 0:1]
        * (
            grad_n
            - jnp.mean(grad_n, axis=1, keepdims=True)
            - nrm * jnp.mean(grad_n * nrm, axis=1, keepdims=True)
        )
    ).astype(BF16)


def grad_q_body(half_scale, q_ref, v0, v1, v2, v3, k0, k1, k2, k3, lane_ref, sub_ref, do_ref, slope_ref, gq_ref):
    width = gq_ref.shape[1]
    dim = width // HEADS
    masks = row_masks(sub_ref, lane_ref)
    for head in range(HEADS):
        at = head * dim
        q = q_ref[:, at : at + dim]
        do = do_ref[:, at : at + dim]
        total = None
        for v_ref, k_ref, mask in zip((v0, v1, v2, v3), (k0, k1, k2, k3), masks):
            k = k_ref[:, at : at + dim]
            half = dot_nt(q, k) * half_scale
            t = jnp.tanh(half)
            slope = (1.0 + t) * ((1.0 + half) - half * t)
            grad_s = (dot_nt(do, v_ref[:, at : at + dim]) * slope).astype(BF16) * mask
            part = dot(grad_s, k)
            total = part if total is None else total + part
        grad = (total * half_scale).astype(BF16).astype(F32)
        gq_ref[:, at : at + dim] = (grad * slope_ref[:, 2 * width + at : 2 * width + at + dim]).astype(BF16)


def grad_kv_sums(half_scale, at, dim, v, k, pairs, sum_v, sum_k):
    for q_ref, do_ref, mask in pairs:
        q = q_ref[:, at : at + dim]
        do = do_ref[:, at : at + dim]
        half = dot_nt(k, q) * half_scale
        t = jnp.tanh(half)
        rise = 1.0 + t
        part_v = dot((half * rise).astype(BF16) * mask, do)
        slope = rise * ((1.0 + half) - half * t)
        grad_s = (dot_nt(v, do) * slope).astype(BF16) * mask
        part_k = dot(grad_s, q)
        sum_v = part_v if sum_v is None else sum_v + part_v
        sum_k = part_k if sum_k is None else sum_k + part_k
    return sum_v, sum_k


def column_masks(sub_ref, lane_ref, blocks):
    key = sub_ref[:, 0:1]
    masks = []
    for b in blocks:
        high = lane_ref[b : b + 1, :]
        low = jnp.floor(high * (1.0 / TIMES)) * TIMES
        masks.append(pair_mask(low, high, key))
    return masks


def grad_kv_near_body(half_scale, v_ref, k_ref, q0, q2, lane_ref, sub_ref, do0, do2, sum_v_ref, sum_k_ref):
    dim = v_ref.shape[1] // HEADS
    masks = column_masks(sub_ref, lane_ref, (0, 2))
    for head in range(HEADS):
        at = head * dim
        sum_v, sum_k = grad_kv_sums(
            half_scale, at, dim, v_ref[:, at : at + dim], k_ref[:, at : at + dim],
            zip((q0, q2), (do0, do2), masks), None, None,
        )
        sum_v_ref[:, at : at + dim] = sum_v
        sum_k_ref[:, at : at + dim] = sum_k


def grad_kv_next_body(half_scale, v_ref, k_ref, q1, lane_ref, sub_ref, do1, near_v, near_k, sum_v_ref, sum_k_ref):
    dim = v_ref.shape[1] // HEADS
    masks = column_masks(sub_ref, lane_ref, (1,))
    for head in range(HEADS):
        at = head * dim
        sum_v, sum_k = grad_kv_sums(
            half_scale, at, dim, v_ref[:, at : at + dim], k_ref[:, at : at + dim],
            zip((q1,), (do1,), masks), near_v[:, at : at + dim], near_k[:, at : at + dim],
        )
        sum_v_ref[:, at : at + dim] = sum_v
        sum_k_ref[:, at : at + dim] = sum_k


def grad_kv_far_body(
    half_scale, v_ref, k_ref, q3, lane_ref, sub_ref, do3, sum_v_ref, sum_k_ref, slope_ref, gu_ref, gq_ref,
    out_ref,
):
    width = gq_ref.shape[1]
    dim = width // HEADS
    masks = column_masks(sub_ref, lane_ref, (3,))
    out_ref[0, :, 0:width] = gu_ref[...]
    out_ref[0, :, 2 * width : 3 * width] = gq_ref[...]
    for head in range(HEADS):
        at = head * dim
        sum_v, sum_k = grad_kv_sums(
            half_scale, at, dim, v_ref[:, at : at + dim], k_ref[:, at : at + dim],
            zip((q3,), (do3,), masks), sum_v_ref[:, at : at + dim], sum_k_ref[:, at : at + dim],
        )
        for first, grad in ((width + at, sum_v), (3 * width + at, sum_k * half_scale)):
            grad = grad.astype(BF16).astype(F32)
            out_ref[0, :, first : first + dim] = (grad * slope_ref[:, first : first + dim]).astype(BF16)


def cut_body(mine_ref, got_ref, own_ref, p1_ref, p2_ref, p3_ref):
    rows = own_ref.shape[0]
    _, _, spot = here()
    for k, ref in enumerate((own_ref, p1_ref, p2_ref, p3_ref)):
        at = pl.ds(pl.multiple_of((spot ^ k) * rows, rows), rows)
        ref[...] = (mine_ref[at, :] + got_ref[at, :].astype(F32)).astype(ref.dtype)


def add_body(own_ref, r1, r2, r3, out_ref):
    out_ref[...] = (
        (own_ref[...].astype(F32) + r1[...].astype(F32)) + (r2[...].astype(F32) + r3[...].astype(F32))
    ).astype(BF16)


def final_body(factor, other, b0, b1, b2, b3, *rest):
    out_hbm, wide_ref, sem = rest[-3:]
    rows = b0.shape[0]
    _, core, spot = here()
    half = 1 - core if other else core
    copies = []
    for k, ref in enumerate((b0, b1, b2, b3)):
        wide_ref[k] = ref[...].astype(F32) * factor
        at = pl.multiple_of((half * 4 + (spot ^ k)) * rows, rows)
        copies.append(pltpu.make_async_copy(wide_ref.at[k], out_hbm.at[pl.ds(at, rows), :], sem.at[k]))
        copies[-1].start()
    for copy in copies:
        copy.wait()


def swap(value, shard_bits, rep_bits=0):
    pairs = [(i, i ^ (shard_bits * 8 + rep_bits)) for i in range(32)]
    return lax.ppermute(value, ("shard", "rep"), pairs)


def by_event(inputs, w_in, grad_out, w_out, dest, slot, slot_user, slot_time):
    x0, dy = inputs[0], grad_out[0]
    events, width = x0.shape
    half_scale = 0.5 / math.sqrt(width // HEADS)
    factor = 1.0 / math.sqrt(32 * events)
    far = functools.partial(pltpu.with_memory_space_constraint, memory_space=pltpu.HBM)
    tie = lax.optimization_barrier
    square = shaped((events, width), BF16)
    square_f32 = shaped((events, width), F32)
    half = shaped((width // 2, width), F32)
    block = shaped((width // 8, width), BF16)
    wide = 2 * events * width

    def project(parts, x):
        return call(
            functools.partial(project_body, parts), [square] * len(parts), [VMEM] * 2, (x, w_near),
            flops=wide * len(parts) * width, moved=3 << 20,
        )

    x1 = swap(x0, 2)
    x2 = swap(x0, 1)
    (info0,) = call(
        pack_body, [shaped((1, 6 * events), jnp.int32)], [HBM] * 4,
        (far(dest), far(slot), far(slot_user), far(slot_time)), moved=1 << 13, scratch=[pltpu.SemaphoreType.DMA((4,))],
    )
    info1 = swap(info0, 2)
    info3 = swap(info0, 3)
    info2 = swap(info0, 1)
    w_near, u0, v0, q0, k0, slope = call(
        project_own_body,
        [shaped(w_in.shape, BF16), square, square, square, square, shaped((events, 4 * width), F32)],
        [HBM] * 2, (far(w_in), far(x0)), flops=wide * 4 * width, moved=6 << 20,
        scratch=[pltpu.VMEM((events, width), BF16), pltpu.SemaphoreType.DMA((5,))],
    )
    v2, q2, k2 = project((1, 2, 3), x2)
    raw0, raw2 = call(
        functools.partial(raw_body, half_scale), [shaped((events, HEADS * events), BF16)] * 2, [VMEM] * 3,
        (q0, k0, k2), flops=wide * 2 * events, moved=2 << 20,
    )
    x1, info1, info2, info3, _ = tie((x1, info1, info2, info3, raw0))
    x3 = swap(x1, 1)
    v1, k1 = project((1, 3), x1)
    (raw1,) = call(
        functools.partial(raw_body, half_scale), [shaped((events, HEADS * events), BF16)], [VMEM] * 2,
        (q0, k1), flops=wide * events, moved=2 << 20,
    )
    info3, _ = tie((info3, raw1))
    lane, sub = call(
        codes_body, [shaped((8, events), F32), shaped((events, 8), F32)], [VMEM] * 4,
        (info0, info1, info2, info3), flops=1 << 26, moved=1 << 20,
    )
    x3_late, _, _ = tie((x3, v1, lane))
    v3, k3 = project((1, 3), x3_late)
    values, keys = (v0, v1, v2, v3), (k0, k1, k2, k3)

    zt, other, nrm, recip = call(
        functools.partial(forward_body, half_scale),
        [shaped((width, events), BF16), shaped(half.shape, BF16), square_f32, shaped((events, 128), F32)],
        [VMEM] * 13, (q0, *values, k3, raw0, raw1, raw2, u0, lane, sub, dy), flops=wide * 4 * events * 3, moved=6 << 20,
        scratch=[pltpu.VMEM((events, width), F32)],
    )
    got = swap(other, 1)
    (mine,) = call(mine_body, [half], [VMEM] * 2, (zt, dy), flops=wide * width, moved=1 << 20, after=(other,))
    do0, gu = call(
        grad_o_body, [square, square], [VMEM] * 6, (u0, dy, w_out, nrm, recip, slope),
        flops=wide * width, moved=4 << 20, after=(other,),
    )
    got, _, _ = tie((got, do0, mine))
    own, p1, p2, p3 = call(
        cut_body, [shaped(block.shape, F32), block, block, block], [VMEM] * 2, (mine, got),
        flops=1 << 20, moved=1 << 20,
    )
    r1, r2, r3 = swap(p1, 0, 1), swap(p2, 2, 0), swap(p3, 2, 1)
    (gq,) = call(
        functools.partial(grad_q_body, half_scale), [square], [VMEM] * 13,
        (q0, *values, *keys, lane, sub, do0, slope), flops=wide * 4 * events * 4, moved=6 << 20, after=(p1, p2, p3),
    )
    (part,) = call(add_body, [block], [VMEM] * 4, (own, r1, r2, r3), flops=1 << 18, moved=1 << 19, after=(gq,))
    r1, r2, r3 = swap(part, 0, 2), swap(part, 0, 4), swap(part, 0, 6)
    do_late, _ = tie((do0, part))
    do2 = swap(do_late, 1)
    do1 = swap(do_late, 2)
    x1_late, x3_late, _ = tie((x1, x3, part))
    (q1,) = project((2,), x1_late)
    (q3,) = project((2,), x3_late)
    sum_v, sum_k = call(
        functools.partial(grad_kv_near_body, half_scale), [square_f32, square_f32], [VMEM] * 8,
        (v0, k0, q0, q2, lane, sub, do0, do2), flops=wide * 4 * events * 3, moved=6 << 20, after=(part,),
    )
    sum_v, sum_k = call(
        functools.partial(grad_kv_next_body, half_scale), [square_f32, square_f32], [VMEM] * 8,
        (v0, k0, q1, lane, sub, do1, sum_v, sum_k),
    )
    (part,) = call(add_body, [block], [VMEM] * 4, (part, r1, r2, r3), flops=1 << 18, moved=1 << 19, after=(sum_v, q1, q3))
    do1, _ = tie((do1, part))
    do3 = swap(do1, 1)
    r1, r2, r3 = swap(part, 0, 1), swap(part, 2, 0), swap(part, 2, 1)
    (grad_rows,) = call(
        functools.partial(grad_kv_far_body, half_scale), [shaped((1, events, 4 * width), BF16)], [VMEM] * 11,
        (v0, k0, q3, lane, sub, do3, sum_v, sum_k, slope, gu, gq),
        flops=wide * 4 * events * 3, moved=8 << 20, after=(part,),
    )
    r1, r2, r3, _ = tie((r1, r2, r3, grad_rows))
    theirs = [swap(b, 1) for b in (part, r1, r2, r3)]
    spread = [pltpu.VMEM((4, width // 8, width), F32), pltpu.SemaphoreType.DMA((4,))]
    (grad_w,) = call(
        functools.partial(final_body, factor, False), [shaped((width, width), F32)], [VMEM] * 4,
        (part, r1, r2, r3), scratch=spread, out_specs=[HBM],
    )
    (grad_w,) = call(
        functools.partial(final_body, factor, True), [shaped((width, width), F32)], [VMEM] * 4 + [HBM],
        (*theirs, grad_w), scratch=spread, out_specs=[HBM], alias={4: 0},
    )
    return grad_rows, grad_w


def on_device(*args):
    events, width = args[0].shape[1:]
    plain = lax.axis_size("shard") == 4 and lax.axis_size("rep") == 8
    if plain and events == 256 and width == 512:
        return by_event(*args)
    return routed(*args)


def solution(mesh):
    return jax.shard_map(
        on_device,
        mesh=mesh,
        in_specs=(
            P("rep", "shard", None),
            P(),
            P("rep", "shard", None),
            P(),
            P("rep", "shard"),
            P("rep", "shard"),
            P("rep", "shard"),
            P("rep", "shard"),
        ),
        out_specs=(P("rep", "shard", None), P()),
        check_vma=False,
    )
```

```python
import functools
import math

import jax
import jax.numpy as jnp
from jax import lax
from jax.experimental import pallas as pl
from jax.experimental.pallas import tpu as pltpu
from jax.sharding import PartitionSpec as P

HEADS = 4
F32 = jnp.float32
BF16 = jnp.bfloat16
TIMES = 512
USERS = 4
VMEM = pl.BlockSpec(memory_space=pltpu.VMEM)
HBM = pl.BlockSpec(memory_space=pltpu.HBM)


def silu_slope(value):
    sigma = jax.nn.sigmoid(value)
    return sigma * (1.0 + value * (1.0 - sigma))


def owner_pass(act, dy_rows, users, times, w_out):
    cap = act.shape[0]
    width = act.shape[1] // 4
    head_dim = width // HEADS
    scale = 1.0 / math.sqrt(head_dim)
    u_part = act[:, :width]
    v_heads = act[:, width : 2 * width].reshape(cap, HEADS, head_dim)
    q_heads = act[:, 2 * width : 3 * width].reshape(cap, HEADS, head_dim)
    k_heads = act[:, 3 * width :].reshape(cap, HEADS, head_dim)
    mask = (
        (users[:, None] == users[None, :])
        & (times[None, :] <= times[:, None])
        & (users[:, None] >= 0)
    )
    scores = (
        jnp.einsum("ihd,jhd->hij", q_heads, k_heads, preferred_element_type=jnp.float32) * scale
    )
    sigma = jax.nn.sigmoid(scores)
    attn = jnp.where(mask[None], scores * sigma, 0.0).astype(jnp.bfloat16)
    out = jnp.einsum("hij,jhd->ihd", attn, v_heads, preferred_element_type=jnp.float32).reshape(
        cap, width
    )
    centred = out - jnp.mean(out, axis=1, keepdims=True)
    recip = lax.rsqrt(jnp.mean(centred * centred, axis=1, keepdims=True) + 1e-05)
    nrm = centred * recip
    u_wide = u_part.astype(jnp.float32)
    zed = (nrm * u_wide).astype(jnp.bfloat16)
    part_w = lax.dot_general(
        zed, dy_rows, (((0,), (0,)), ((), ())), preferred_element_type=jnp.float32
    )
    dzed = lax.dot_general(
        dy_rows, w_out, (((1,), (1,)), ((), ())), preferred_element_type=jnp.float32
    )
    grad_u = dzed * nrm
    grad_n = dzed * u_wide
    grad_o = recip * (
        grad_n
        - jnp.mean(grad_n, axis=1, keepdims=True)
        - nrm * jnp.mean(grad_n * nrm, axis=1, keepdims=True)
    )
    grad_o = grad_o.astype(jnp.bfloat16).reshape(cap, HEADS, head_dim)
    grad_a = jnp.einsum("ihd,jhd->hij", grad_o, v_heads, preferred_element_type=jnp.float32)
    grad_v = jnp.einsum("hij,ihd->jhd", attn, grad_o, preferred_element_type=jnp.float32)
    grad_s = jnp.where(
        mask[None], grad_a * sigma * (1.0 + scores * (1.0 - sigma)) * scale, 0.0
    ).astype(jnp.bfloat16)
    grad_q = jnp.einsum("hij,jhd->ihd", grad_s, k_heads, preferred_element_type=jnp.float32)
    grad_k = jnp.einsum("hij,ihd->jhd", grad_s, q_heads, preferred_element_type=jnp.float32)
    grad_act = jnp.concatenate(
        [
            grad_u,
            grad_v.reshape(cap, width),
            grad_q.reshape(cap, width),
            grad_k.reshape(cap, width),
        ],
        axis=1,
    ).astype(jnp.bfloat16)
    return (lax.optimization_barrier(grad_act), part_w)


def routed(inputs, w_in, grad_out, w_out, dest, slot, slot_user, slot_time):
    shards = lax.axis_size("shard")
    groups = lax.axis_size("rep")
    per_dev = inputs.shape[1]
    width = inputs.shape[2]
    slots = 2 * per_dev // shards
    cap = shards * slots
    rows = inputs[0]
    flat = dest[0] * slots + slot[0]
    dy_buf = (
        jnp.zeros((cap, width), jnp.bfloat16)
        .at[flat]
        .set(grad_out[0])
        .reshape(shards, slots, width)
    )
    proj = jnp.dot(rows, w_in, preferred_element_type=jnp.float32)
    act = (proj * jax.nn.sigmoid(proj)).astype(jnp.bfloat16)
    act_buf = (
        jnp.zeros((cap, 4 * width), jnp.bfloat16)
        .at[flat]
        .set(act)
        .reshape(shards, slots, 4 * width)
    )
    got_act, got_dy = (
        lax.all_to_all(act_buf, "shard", split_axis=0, concat_axis=0, tiled=True),
        lax.all_to_all(dy_buf, "shard", split_axis=0, concat_axis=0, tiled=True),
    )
    owner_act = got_act.reshape(cap, 4 * width)
    grad_act, part_w = owner_pass(
        owner_act, got_dy.reshape(cap, width), slot_user[0], slot_time[0], w_out
    )
    back = lax.all_to_all(
        grad_act.reshape(shards, slots, 4 * width), "shard", split_axis=0, concat_axis=0, tiled=True
    )
    mine = back.reshape(cap, 4 * width)[flat]
    grad_rows = (mine.astype(jnp.float32) * silu_slope(proj)).astype(jnp.bfloat16)
    factor = 1.0 / math.sqrt(groups * shards * per_dev)
    summed = lax.psum(part_w, ("shard", "rep"))
    return (grad_rows[None], summed * factor)


def dot(a, b):
    return jnp.dot(a, b, preferred_element_type=F32)


def dot_nt(a, b):
    return lax.dot_general(a, b, (((1,), (1,)), ((), ())), preferred_element_type=F32)


def here():
    me, rep = lax.axis_index("shard"), lax.axis_index("rep")
    return me, lax.rem(me, 2), lax.div(me, 2) * 2 + lax.rem(rep, 2)


def call(body, outs, specs, args, flops=0, moved=0, scratch=(), after=(), out_specs=None, alias=None):
    if after:
        last, *_ = lax.optimization_barrier((args[-1], *after))
        args = (*args[:-1], last)
    return pl.pallas_call(
        body,
        out_shape=outs,
        in_specs=specs,
        out_specs=out_specs or [VMEM] * len(outs),
        scratch_shapes=list(scratch),
        input_output_aliases=alias or {},
        compiler_params=pltpu.CompilerParams(vmem_limit_bytes=16 << 20),
        cost_estimate=pl.CostEstimate(flops=1 << 10, bytes_accessed=1 << 10, transcendentals=0),
    )(*args)


def shaped(shape, kind):
    return jax.ShapeDtypeStruct(shape, kind)


def silu_of(h):
    half = 0.5 * h
    t = jnp.tanh(half)
    return half + half * t, t


def project_own_body(w_hbm, x_hbm, w_ref, u_ref, v_ref, q_ref, k_ref, slope_ref, x_ref, sem):
    width = u_ref.shape[1]
    copies = [pltpu.make_async_copy(x_hbm, x_ref, sem.at[4])]
    for i in range(4):
        block = pl.ds(i * width, width)
        copies.append(pltpu.make_async_copy(w_hbm.at[:, block], w_ref.at[:, block], sem.at[i]))
    for copy in copies:
        copy.start()
    copies[0].wait()
    x = x_ref[...]
    for i, ref in enumerate((u_ref, v_ref, q_ref, k_ref)):
        copies[i + 1].wait()
        for col in range(0, width, 256):
            first = i * width + col
            act, t = silu_of(dot(x, w_ref[:, first : first + 256]))
            slope_ref[:, first : first + 256] = 0.5 * ((1.0 + t) + act * (1.0 - t))
            ref[:, col : col + 256] = act.astype(BF16)


def project_body(parts, x_ref, w_ref, *out_refs):
    width = x_ref.shape[1]
    x = x_ref[...]
    for part, ref in zip(parts, out_refs):
        for col in range(0, width, 256):
            first = part * width + col
            act, _ = silu_of(dot(x, w_ref[:, first : first + 256]))
            ref[:, col : col + 256] = act.astype(BF16)


def pack_body(dest_ref, slot_ref, user_ref, time_ref, out_ref, sem):
    first, copies = 0, []
    for i, ref in enumerate((dest_ref, slot_ref, user_ref, time_ref)):
        copies.append(pltpu.make_async_copy(ref, out_ref.at[:, first : first + ref.shape[1]], sem.at[i]))
        first += ref.shape[1]
    for copy in copies:
        copy.start()
    for copy in copies:
        copy.wait()


def codes_body(i0, i1, i2, i3, lane_ref, sub_ref):
    infos = (i0, i1, i2, i3)
    me, _, _ = here()
    ids = (me, me ^ 2, me ^ 1, me ^ 3)
    events = lane_ref.shape[1]
    slots = events // 2
    row8 = lax.broadcasted_iota(jnp.int32, (8, slots), 0)
    down = lax.broadcasted_iota(jnp.int32, (slots, events), 0)
    rows = []
    for b in range(4):
        flat = infos[b][:, 0:events] * slots + infos[b][:, events : 2 * events]
        tables, hits = [], []
        for p in range(4):
            at = pl.multiple_of(2 * events + ids[b] * slots, slots)
            user = infos[p][:, pl.ds(at, slots)]
            at = pl.multiple_of(4 * events + ids[b] * slots, slots)
            code = (ids[p] * USERS + user) * TIMES + infos[p][:, pl.ds(at, slots)]
            tables.append(jnp.where(row8 == 0, code >> 6, code & 63).astype(F32).astype(BF16))
            hits.append(jnp.where(down == flat - ids[p] * slots, 1.0, 0.0).astype(BF16))
        total = dot(jnp.concatenate(tables, axis=1), jnp.concatenate(hits, axis=0))
        rows.append(total[0:1] * 64.0 + total[1:2])
    codes = jnp.concatenate(rows + rows, axis=0)
    lane_ref[...] = codes
    sub_ref[...] = codes.T


def pair_mask(low, high, key):
    return jnp.where((key >= low) & (key <= high), 1.0, 0.0).astype(BF16)


def raw_body(half_scale, q_ref, *refs):
    events = q_ref.shape[0]
    dim = q_ref.shape[1] // HEADS
    count = len(refs) // 2
    for head in range(HEADS):
        at = head * dim
        q = q_ref[:, at : at + dim]
        for k_ref, raw_ref in zip(refs[:count], refs[count:]):
            half = dot_nt(q, k_ref[:, at : at + dim]) * half_scale
            raw_ref[:, head * events : (head + 1) * events] = (half + half * jnp.tanh(half)).astype(BF16)


def row_masks(sub_ref, lane_ref):
    high = sub_ref[:, 0:1]
    low = jnp.floor(high * (1.0 / TIMES)) * TIMES
    return [pair_mask(low, high, lane_ref[b : b + 1, :]) for b in range(4)]


def forward_body(
    half_scale, q_ref, v0, v1, v2, v3, k3, raw0, raw1, raw2, u_ref, lane_ref, sub_ref, dy_ref,
    zt_ref, other_ref, nrm_ref, recip_ref, o_ref,
):
    events = q_ref.shape[0]
    dim = u_ref.shape[1] // HEADS
    masks = row_masks(sub_ref, lane_ref)
    for head in range(HEADS):
        at = head * dim
        q = q_ref[:, at : at + dim]
        total = None
        for v_ref, k_ref, raw_ref, mask in zip((v0, v1, v2, v3), (None, None, None, k3), (raw0, raw1, raw2, None), masks):
            if raw_ref is None:
                half = dot_nt(q, k_ref[:, at : at + dim]) * half_scale
                attn = (half + half * jnp.tanh(half)).astype(BF16)
            else:
                attn = raw_ref[:, head * events : (head + 1) * events]
            part = dot(attn * mask, v_ref[:, at : at + dim])
            total = part if total is None else total + part
        o_ref[:, at : at + dim] = total
    out = o_ref[...]
    centred = out - jnp.mean(out, axis=1, keepdims=True)
    recip = lax.rsqrt(jnp.mean(centred * centred, axis=1, keepdims=True) + 1e-05)
    nrm = centred * recip
    nrm_ref[...] = nrm
    recip_ref[...] = jnp.broadcast_to(recip, recip_ref.shape)
    zt_ref[...] = (nrm * u_ref[...].astype(F32)).T.astype(BF16)
    rows = other_ref.shape[0]
    _, core, _ = here()
    at = pl.ds(pl.multiple_of((1 - core) * rows, rows), rows)
    other_ref[...] = dot(zt_ref[at, :], dy_ref[...]).astype(BF16)


def mine_body(zt_ref, dy_ref, mine_ref):
    rows = mine_ref.shape[0]
    _, core, _ = here()
    mine_ref[...] = dot(zt_ref[pl.ds(pl.multiple_of(core * rows, rows), rows), :], dy_ref[...])


def grad_o_body(u_ref, dy_ref, w_out_ref, nrm_ref, recip_ref, slope_ref, do_ref, gu_ref):
    width = u_ref.shape[1]
    dzed = dot_nt(dy_ref[...], w_out_ref[...])
    nrm = nrm_ref[...]
    gu_ref[...] = ((dzed * nrm).astype(BF16).astype(F32) * slope_ref[:, :width]).astype(BF16)
    grad_n = dzed * u_ref[...].astype(F32)
    do_ref[...] = (
        recip_ref[:, 0:1]
        * (
            grad_n
            - jnp.mean(grad_n, axis=1, keepdims=True)
            - nrm * jnp.mean(grad_n * nrm, axis=1, keepdims=True)
        )
    ).astype(BF16)


def grad_q_body(half_scale, q_ref, v0, v1, v2, v3, k0, k1, k2, k3, lane_ref, sub_ref, do_ref, slope_ref, gq_ref):
    width = gq_ref.shape[1]
    dim = width // HEADS
    masks = row_masks(sub_ref, lane_ref)
    for head in range(HEADS):
        at = head * dim
        q = q_ref[:, at : at + dim]
        do = do_ref[:, at : at + dim]
        total = None
        for v_ref, k_ref, mask in zip((v0, v1, v2, v3), (k0, k1, k2, k3), masks):
            k = k_ref[:, at : at + dim]
            half = dot_nt(q, k) * half_scale
            t = jnp.tanh(half)
            slope = (1.0 + t) * ((1.0 + half) - half * t)
            grad_s = (dot_nt(do, v_ref[:, at : at + dim]) * slope).astype(BF16) * mask
            part = dot(grad_s, k)
            total = part if total is None else total + part
        grad = (total * half_scale).astype(BF16).astype(F32)
        gq_ref[:, at : at + dim] = (grad * slope_ref[:, 2 * width + at : 2 * width + at + dim]).astype(BF16)


def grad_kv_sums(half_scale, at, dim, v, k, pairs, sum_v, sum_k):
    for q_ref, do_ref, mask in pairs:
        q = q_ref[:, at : at + dim]
        do = do_ref[:, at : at + dim]
        half = dot_nt(k, q) * half_scale
        t = jnp.tanh(half)
        rise = 1.0 + t
        part_v = dot((half * rise).astype(BF16) * mask, do)
        slope = rise * ((1.0 + half) - half * t)
        grad_s = (dot_nt(v, do) * slope).astype(BF16) * mask
        part_k = dot(grad_s, q)
        sum_v = part_v if sum_v is None else sum_v + part_v
        sum_k = part_k if sum_k is None else sum_k + part_k
    return sum_v, sum_k


def column_masks(sub_ref, lane_ref, blocks):
    key = sub_ref[:, 0:1]
    masks = []
    for b in blocks:
        high = lane_ref[b : b + 1, :]
        low = jnp.floor(high * (1.0 / TIMES)) * TIMES
        masks.append(pair_mask(low, high, key))
    return masks


def grad_kv_near_body(half_scale, v_ref, k_ref, q0, q2, lane_ref, sub_ref, do0, do2, sum_v_ref, sum_k_ref):
    dim = v_ref.shape[1] // HEADS
    masks = column_masks(sub_ref, lane_ref, (0, 2))
    for head in range(HEADS):
        at = head * dim
        sum_v, sum_k = grad_kv_sums(
            half_scale, at, dim, v_ref[:, at : at + dim], k_ref[:, at : at + dim],
            zip((q0, q2), (do0, do2), masks), None, None,
        )
        sum_v_ref[:, at : at + dim] = sum_v
        sum_k_ref[:, at : at + dim] = sum_k


def grad_kv_next_body(half_scale, v_ref, k_ref, q1, lane_ref, sub_ref, do1, near_v, near_k, sum_v_ref, sum_k_ref):
    dim = v_ref.shape[1] // HEADS
    masks = column_masks(sub_ref, lane_ref, (1,))
    for head in range(HEADS):
        at = head * dim
        sum_v, sum_k = grad_kv_sums(
            half_scale, at, dim, v_ref[:, at : at + dim], k_ref[:, at : at + dim],
            zip((q1,), (do1,), masks), near_v[:, at : at + dim], near_k[:, at : at + dim],
        )
        sum_v_ref[:, at : at + dim] = sum_v
        sum_k_ref[:, at : at + dim] = sum_k


def grad_kv_far_body(
    half_scale, v_ref, k_ref, q3, lane_ref, sub_ref, do3, sum_v_ref, sum_k_ref, slope_ref, gu_ref, gq_ref,
    out_ref,
):
    width = gq_ref.shape[1]
    dim = width // HEADS
    masks = column_masks(sub_ref, lane_ref, (3,))
    out_ref[0, :, 0:width] = gu_ref[...]
    out_ref[0, :, 2 * width : 3 * width] = gq_ref[...]
    for head in range(HEADS):
        at = head * dim
        sum_v, sum_k = grad_kv_sums(
            half_scale, at, dim, v_ref[:, at : at + dim], k_ref[:, at : at + dim],
            zip((q3,), (do3,), masks), sum_v_ref[:, at : at + dim], sum_k_ref[:, at : at + dim],
        )
        for first, grad in ((width + at, sum_v), (3 * width + at, sum_k * half_scale)):
            grad = grad.astype(BF16).astype(F32)
            out_ref[0, :, first : first + dim] = (grad * slope_ref[:, first : first + dim]).astype(BF16)


def cut_body(mine_ref, got_ref, own_ref, p1_ref, p2_ref, p3_ref):
    rows = own_ref.shape[0]
    _, _, spot = here()
    for k, ref in enumerate((own_ref, p1_ref, p2_ref, p3_ref)):
        at = pl.ds(pl.multiple_of((spot ^ k) * rows, rows), rows)
        ref[...] = (mine_ref[at, :] + got_ref[at, :].astype(F32)).astype(ref.dtype)


def add_body(own_ref, r1, r2, r3, out_ref):
    out_ref[...] = (
        (own_ref[...].astype(F32) + r1[...].astype(F32)) + (r2[...].astype(F32) + r3[...].astype(F32))
    ).astype(BF16)


def final_body(factor, places, *refs):
    count = len(places)
    out_hbm, wide_ref, sem = refs[-3:]
    rows = refs[0].shape[0]
    _, core, spot = here()
    copies = []
    for i, ((other, k), ref) in enumerate(zip(places, refs[:count])):
        half = 1 - core if other else core
        wide_ref[i] = ref[...].astype(F32) * factor
        at = pl.multiple_of((half * 4 + (spot ^ k)) * rows, rows)
        copies.append(pltpu.make_async_copy(wide_ref.at[i], out_hbm.at[pl.ds(at, rows), :], sem.at[i]))
        copies[-1].start()
    for copy in copies:
        copy.wait()


def swap(value, shard_bits, rep_bits=0):
    pairs = [(i, i ^ (shard_bits * 8 + rep_bits)) for i in range(32)]
    return lax.ppermute(value, ("shard", "rep"), pairs)


def by_event(inputs, w_in, grad_out, w_out, dest, slot, slot_user, slot_time):
    x0, dy = inputs[0], grad_out[0]
    events, width = x0.shape
    half_scale = 0.5 / math.sqrt(width // HEADS)
    factor = 1.0 / math.sqrt(32 * events)
    far = functools.partial(pltpu.with_memory_space_constraint, memory_space=pltpu.HBM)
    tie = lax.optimization_barrier
    square = shaped((events, width), BF16)
    square_f32 = shaped((events, width), F32)
    half = shaped((width // 2, width), F32)
    block = shaped((width // 8, width), BF16)
    wide = 2 * events * width

    def project(parts, x):
        return call(
            functools.partial(project_body, parts), [square] * len(parts), [VMEM] * 2, (x, w_near),
            flops=wide * len(parts) * width, moved=3 << 20,
        )

    x1 = swap(x0, 2)
    x2 = swap(x0, 1)
    (info0,) = call(
        pack_body, [shaped((1, 6 * events), jnp.int32)], [HBM] * 4,
        (far(dest), far(slot), far(slot_user), far(slot_time)), moved=1 << 13, scratch=[pltpu.SemaphoreType.DMA((4,))],
    )
    info1 = swap(info0, 2)
    info3 = swap(info0, 3)
    info2 = swap(info0, 1)
    w_near, u0, v0, q0, k0, slope = call(
        project_own_body,
        [shaped(w_in.shape, BF16), square, square, square, square, shaped((events, 4 * width), F32)],
        [HBM] * 2, (far(w_in), far(x0)), flops=wide * 4 * width, moved=6 << 20,
        scratch=[pltpu.VMEM((events, width), BF16), pltpu.SemaphoreType.DMA((5,))],
    )
    v2, q2, k2 = project((1, 2, 3), x2)
    raw0, raw2 = call(
        functools.partial(raw_body, half_scale), [shaped((events, HEADS * events), BF16)] * 2, [VMEM] * 3,
        (q0, k0, k2), flops=wide * 2 * events, moved=2 << 20,
    )
    x1, info1, info2, info3, _ = tie((x1, info1, info2, info3, raw0))
    x3 = swap(x1, 1)
    v1, k1 = project((1, 3), x1)
    (raw1,) = call(
        functools.partial(raw_body, half_scale), [shaped((events, HEADS * events), BF16)], [VMEM] * 2,
        (q0, k1), flops=wide * events, moved=2 << 20,
    )
    info3, _ = tie((info3, raw1))
    lane, sub = call(
        codes_body, [shaped((8, events), F32), shaped((events, 8), F32)], [VMEM] * 4,
        (info0, info1, info2, info3), flops=1 << 26, moved=1 << 20,
    )
    x3_late, _, _ = tie((x3, v1, lane))
    v3, k3 = project((1, 3), x3_late)
    values, keys = (v0, v1, v2, v3), (k0, k1, k2, k3)

    zt, other, nrm, recip = call(
        functools.partial(forward_body, half_scale),
        [shaped((width, events), BF16), shaped(half.shape, BF16), square_f32, shaped((events, 128), F32)],
        [VMEM] * 13, (q0, *values, k3, raw0, raw1, raw2, u0, lane, sub, dy), flops=wide * 4 * events * 3, moved=6 << 20,
        scratch=[pltpu.VMEM((events, width), F32)],
    )
    got = swap(other, 1)
    (mine,) = call(mine_body, [half], [VMEM] * 2, (zt, dy), flops=wide * width, moved=1 << 20, after=(other,))
    do0, gu = call(
        grad_o_body, [square, square], [VMEM] * 6, (u0, dy, w_out, nrm, recip, slope),
        flops=wide * width, moved=4 << 20, after=(other,),
    )
    got, _, _ = tie((got, do0, mine))
    own, p1, p2, p3 = call(
        cut_body, [shaped(block.shape, F32), block, block, block], [VMEM] * 2, (mine, got),
        flops=1 << 20, moved=1 << 20,
    )
    r1, r2, r3 = swap(p1, 0, 1), swap(p2, 2, 0), swap(p3, 2, 1)
    (gq,) = call(
        functools.partial(grad_q_body, half_scale), [square], [VMEM] * 13,
        (q0, *values, *keys, lane, sub, do0, slope), flops=wide * 4 * events * 4, moved=6 << 20, after=(p1, p2, p3),
    )
    (part,) = call(add_body, [block], [VMEM] * 4, (own, r1, r2, r3), flops=1 << 18, moved=1 << 19, after=(gq,))
    r1, r2, r3 = swap(part, 0, 2), swap(part, 0, 4), swap(part, 0, 6)
    do_late, _ = tie((do0, part))
    do2 = swap(do_late, 1)
    do1 = swap(do_late, 2)
    x1_late, x3_late, _ = tie((x1, x3, part))
    (q1,) = project((2,), x1_late)
    (q3,) = project((2,), x3_late)
    sum_v, sum_k = call(
        functools.partial(grad_kv_near_body, half_scale), [square_f32, square_f32], [VMEM] * 8,
        (v0, k0, q0, q2, lane, sub, do0, do2), flops=wide * 4 * events * 3, moved=6 << 20, after=(part,),
    )
    sum_v, sum_k = call(
        functools.partial(grad_kv_next_body, half_scale), [square_f32, square_f32], [VMEM] * 8,
        (v0, k0, q1, lane, sub, do1, sum_v, sum_k),
    )
    (part,) = call(add_body, [block], [VMEM] * 4, (part, r1, r2, r3), flops=1 << 18, moved=1 << 19, after=(sum_v, q1, q3))
    do1, _ = tie((do1, part))
    do3 = swap(do1, 1)
    r1, r2, r3 = swap(part, 0, 1), swap(part, 2, 0), swap(part, 2, 1)
    (grad_rows,) = call(
        functools.partial(grad_kv_far_body, half_scale), [shaped((1, events, 4 * width), BF16)], [VMEM] * 11,
        (v0, k0, q3, lane, sub, do3, sum_v, sum_k, slope, gu, gq),
        flops=wide * 4 * events * 3, moved=8 << 20, after=(part,),
    )
    r1, r2, r3, _ = tie((r1, r2, r3, grad_rows))
    theirs = [swap(b, 1) for b in (part, r1, r2, r3)]
    def spread(count):
        return [pltpu.VMEM((count, width // 8, width), F32), pltpu.SemaphoreType.DMA((count,))]

    first = ((False, 0), (False, 1), (False, 2), (False, 3), (True, 0))
    (grad_w,) = call(
        functools.partial(final_body, factor, first), [shaped((width, width), F32)], [VMEM] * 5,
        (part, r1, r2, r3, theirs[0]), scratch=spread(5), out_specs=[HBM],
    )
    last = ((True, 1), (True, 2), (True, 3))
    (grad_w,) = call(
        functools.partial(final_body, factor, last), [shaped((width, width), F32)], [VMEM] * 3 + [HBM],
        (*theirs[1:], grad_w), scratch=spread(3), out_specs=[HBM], alias={3: 0},
    )
    return grad_rows, grad_w


def on_device(*args):
    events, width = args[0].shape[1:]
    plain = lax.axis_size("shard") == 4 and lax.axis_size("rep") == 8
    if plain and events == 256 and width == 512:
        return by_event(*args)
    return routed(*args)


def solution(mesh):
    return jax.shard_map(
        on_device,
        mesh=mesh,
        in_specs=(
            P("rep", "shard", None),
            P(),
            P("rep", "shard", None),
            P(),
            P("rep", "shard"),
            P("rep", "shard"),
            P("rep", "shard"),
            P("rep", "shard"),
        ),
        out_specs=(P("rep", "shard", None), P()),
        check_vma=False,
    )
```
